32 devices in a mesh: sector: 8 (over z, x), band: 4 (over y, core).
Axes of the slice: x: 2, y: 2, z: 4, core: 2. Of those that a mesh axis runs over, the one named last changes fastest.
Arguments:
- queries: bfloat16 [128, 256, 256], P('sector', 'band'), may hold values from -6 to 6
- norm_gain: float32 [256], replicated, may hold values from 0.5 to 1.5
- w_query: bfloat16 [256, 256], replicated, may hold values from -0.375 to 0.375
- w_key: bfloat16 [256, 256], replicated, may hold values from -0.375 to 0.375
- w_value: bfloat16 [256, 256], replicated, may hold values from -0.375 to 0.375
- w_out: bfloat16 [256, 256], replicated, may hold values from -0.375 to 0.375
- features: bfloat16 [65536, 256], P(('sector', 'band')), may hold values from -160 to 160
- visible: int32 [128, 256, 3], P('sector', 'band'), may hold values from 0 to 3071, as said below
- live: int32 [128, 256, 3], P('sector', 'band'), may hold values from 0 to 1, as said below
Outputs:
- attended: bfloat16 [128, 256, 256], P('sector', 'band')
The draws below stay inside these ranges and needn't reach their ends.
Inputs may be any that keep to these rules, and one draw needn't show every extreme that they name: `visible`: on each device (s, j), the 3072 entries name every code from 0 to 3071 exactly once. `live`: 1 marks an entry that contributes, 0 one that does not.
All inputs are finite; a program needn't handle non-finite values.
Results may differ from the reference program's by a relative error of at most 0.0025.
The reference program's roundings to bfloat16 on the way count: a program that leaves them out, or rounds other values in their place, can miss the bound.
Values may be sent and summed in bfloat16 or wider, within the bound.
No kernel may reach another device: no remote copies, remote signals or barrier semaphores. Data moves between devices by JAX's collectives and lax.ppermute only.
A program may use at most 128 MiB of HBM per device.

```python
import jax
import jax.numpy as jnp
from jax import lax

D = 256
HEADS = 8
HD = 32
QA = 16
QR = 64
TOP = 3
BLK_DEV = 8
KB = 1024
CAP = 128
NSA = 128
NBR = 256
KEYS = 65536
N_SECTOR = 8
N_BAND = 4


def draw_features(key, part):
    values_drawn = jnp.clip(jax.random.normal(key, (KEYS, D), jnp.float32), -4.0, 4.0)
    return values_drawn.astype(jnp.bfloat16)


def draw_visible(key, part):
    sectors = NSA // QA
    bands = NBR // QR
    entry_total = QA * QR * TOP
    device_keys = jax.random.split(key, sectors * bands)
    orders = jax.vmap(lambda device_key: jax.random.permutation(device_key, entry_total))(device_keys)
    orders = orders.reshape(sectors, bands, QA, QR, TOP).transpose(0, 2, 1, 3, 4)
    return orders.reshape(NSA, NBR, TOP).astype(jnp.int32)


def draw_live(key, part):
    range_index = jnp.arange(NBR, dtype=jnp.int32)
    threshold = 900 - 600 * range_index // NBR
    ticket = jax.random.randint(key, (NSA, NBR, TOP), 0, 1000)
    return (ticket < threshold[None, :, None]).astype(jnp.int32)


def steps_of(rng, extent, shards, smallest, largest):
    factor_of, own = 1.0, jax.random.fold_in(rng, 6)
    for position, shards_of in shards:
        steps = jnp.exp(jax.random.uniform(jax.random.fold_in(own, position), (shards_of,), jnp.float32, smallest / len(shards), largest / len(shards)))
        factor_of = factor_of * jnp.repeat(steps, extent[position] // shards_of).reshape([-1 if axis == position else 1 for axis in range(len(extent))])
    return factor_of


def gaussian(own_key, shape, scale, bound, cuts=(), kind=jnp.bfloat16):
    gain = steps_of(own_key, shape, cuts, -0.22, 0.18) if cuts else 1.0
    values = jax.random.normal(own_key, shape, jnp.float32) * scale * gain
    return jnp.minimum(jnp.maximum(values, -bound), bound).astype(kind)


def setup_inputs(seed: int = 0) -> dict:
    keys = jax.random.split(jax.random.key(seed), 10)
    queries = gaussian(keys[0], (NSA, NBR, D), 1.0, 6.0, ((0, 8), (1, 4)))
    norm_gain = jnp.clip(jax.random.uniform(keys[1], (D,), jnp.float32, 0.5, 1.5), 0.5, 1.5)
    w_query = gaussian(keys[2], (D, D), D ** -0.5, 0.375)
    w_key = gaussian(keys[3], (D, D), D ** -0.5, 0.375)
    w_value = gaussian(keys[4], (D, D), D ** -0.5, 0.375)
    w_out = gaussian(keys[5], (D, D), D ** -0.5, 0.375)
    features = draw_features(jax.random.fold_in(keys[9], 71), 0)
    visible = draw_visible(jax.random.fold_in(keys[9], 71), 0)
    live = draw_live(jax.random.fold_in(keys[9], 71), 0)
    return dict(queries=queries, norm_gain=norm_gain, w_query=w_query, w_key=w_key, w_value=w_value, w_out=w_out, features=features, visible=visible, live=live)


def attend(rows, block):
    row_count = rows.shape[0]
    key_count = block.shape[0]
    query_heads = rows.reshape(row_count, HEADS, HD).transpose(1, 0, 2)
    key_heads = block[:, :D].reshape(key_count, HEADS, HD).transpose(1, 0, 2)
    value_heads = block[:, D:].reshape(key_count, HEADS, HD).transpose(1, 0, 2)

    def one_head(triple):
        query_head, key_head, value_head = triple
        scores = jnp.dot(query_head, key_head.T, preferred_element_type=jnp.float32) * HD ** (-0.5)
        peak = lax.optimization_barrier(jnp.max(scores, axis=-1, keepdims=True))
        expo = jnp.exp(scores - peak)
        weights = (expo / lax.optimization_barrier(jnp.sum(expo, axis=-1, keepdims=True))).astype(jnp.bfloat16)
        return jnp.dot(weights, value_head, preferred_element_type=jnp.float32).astype(jnp.bfloat16)
    heads_out = lax.map(one_head, (query_heads, key_heads, value_heads))
    return heads_out.transpose(1, 0, 2).reshape(row_count, D)

def reference(queries, norm_gain, w_query, w_key, w_value, w_out, features, visible, live):
    sectors = N_SECTOR
    bands = N_BAND
    query_count = QA * QR
    slot_total = 3 * BLK_DEV * CAP
    values_in = queries.astype(jnp.float32)
    average = lax.optimization_barrier(jnp.mean(values_in, axis=-1, keepdims=True))
    spread = lax.optimization_barrier(jnp.mean((values_in - average) ** 2, axis=-1, keepdims=True))
    normed = ((values_in - average) * lax.rsqrt(spread + 1e-05) * norm_gain).astype(jnp.bfloat16)
    projected = jnp.dot(normed.reshape(-1, D), w_query, preferred_element_type=jnp.float32).astype(jnp.bfloat16)
    w_both = jnp.concatenate([w_key, w_value], axis=1)
    key_values = jnp.dot(features, w_both, preferred_element_type=jnp.float32).astype(jnp.bfloat16)
    key_values = key_values.reshape(sectors, BLK_DEV, KB, 2 * D)

    def per_device(array, last):
        return array.reshape(sectors, QA, bands, QR, last).transpose(0, 2, 1, 3, 4).reshape(sectors, bands, query_count * last)
    proj_dev = per_device(projected.reshape(sectors * QA, bands * QR, D), D).reshape(sectors, bands, query_count, D)
    codes_dev = per_device(visible, TOP)
    live_dev = per_device(live, TOP).reshape(sectors, bands, query_count, TOP)

    def per_sector(inputs):
        sector_index, rows, slot_codes, live_rows = inputs

        def fill(device_rows, device_codes):
            empty = jnp.zeros((slot_total, D), jnp.bfloat16)
            return empty.at[device_codes].set(jnp.repeat(device_rows, TOP, axis=0))
        buffers = jax.vmap(fill)(rows, slot_codes).reshape(bands, 3, BLK_DEV, CAP, D)
        buffers = buffers.transpose(1, 2, 0, 3, 4).reshape(3 * BLK_DEV, bands * CAP, D)
        owners = (sector_index + jnp.arange(3, dtype=jnp.int32) - 1) % sectors
        blocks = key_values[owners].reshape(3 * BLK_DEV, KB, 2 * D)
        results = lax.map(lambda pair: attend(pair[0], pair[1]), (buffers, blocks))
        results = results.reshape(3, BLK_DEV, bands, CAP, D).transpose(2, 0, 1, 3, 4).reshape(bands, slot_total, D)
        picked = jax.vmap(lambda table, device_codes: table[device_codes])(results, slot_codes)
        picked = picked.reshape(bands, query_count, TOP, D).astype(jnp.float32)
        summed = lax.optimization_barrier(jnp.sum(picked * live_rows[..., None].astype(jnp.float32), axis=2))
        return summed.astype(jnp.bfloat16)
    summed = lax.map(per_sector, (jnp.arange(sectors, dtype=jnp.int32), proj_dev, codes_dev, live_dev))
    summed = summed.reshape(sectors, bands, QA, QR, D).transpose(0, 2, 1, 3, 4).reshape(-1, D)
    final = jnp.dot(summed, w_out, preferred_element_type=jnp.float32) + queries.reshape(-1, D).astype(jnp.float32)
    return final.astype(jnp.bfloat16).reshape(sectors * QA, bands * QR, D)
```

```python
import functools

import jax
import jax.numpy as jnp
from jax import lax
from jax.experimental import pallas as pl
from jax.experimental.pallas import tpu as pltpu
from jax.sharding import PartitionSpec as P

HEADS = 8
BLK_DEV = 8
CAP = 128
LOG2_E = 1.4426950408889634
VMEM_BYTES = 48 << 20


def params():
    return pltpu.CompilerParams(vmem_limit_bytes=VMEM_BYTES)


def whole(shape):
    return pl.BlockSpec(shape, lambda *_: (0,) * len(shape))


def shifted(block, axis, distance):
    count = lax.axis_size(axis)
    return lax.ppermute(block, axis, [(i, (i + distance) % count) for i in range(count)])


def swapped(block, axis, bit):
    count = lax.axis_size(axis)
    return lax.ppermute(block, axis, [(i, i ^ bit) for i in range(count)])


def fill_slots(codes_ref, rows, out_ref, group):
    per_group = BLK_DEV * CAP
    tile = 2 * CAP
    queries = rows.shape[0]
    for step in range(per_group // tile):
        slot = lax.broadcasted_iota(jnp.int32, (tile, queries), 0) + (group * per_group + step * tile)
        hit = slot == codes_ref[0:1, :]
        for entry in range(1, codes_ref.shape[0]):
            hit = hit | (slot == codes_ref[entry:entry + 1, :])
        pick = jnp.where(hit, 1.0, 0.0).astype(jnp.bfloat16)
        got = jnp.dot(pick, rows, preferred_element_type=jnp.float32).astype(jnp.bfloat16)
        out_ref[2 * step:2 * step + 2] = got.reshape(2, CAP, got.shape[1])


def project_kernel(codes_ref, queries_ref, gain_ref, weight_ref, rows_ref, slots_ref):
    values = queries_ref[...].astype(jnp.float32)
    average = jnp.mean(values, axis=-1, keepdims=True)
    centred = values - average
    spread = jnp.mean(centred * centred, axis=-1, keepdims=True)
    normed = (centred * lax.rsqrt(spread + 1e-05) * gain_ref[...]).astype(jnp.bfloat16)
    rows = jnp.dot(normed, weight_ref[...], preferred_element_type=jnp.float32).astype(jnp.bfloat16)
    rows_ref[...] = rows
    fill_slots(codes_ref, rows, slots_ref, 2)


def project(codes, queries, gain, weight):
    count, width = queries.shape
    return pl.pallas_call(
        project_kernel,
        out_shape=(
            jax.ShapeDtypeStruct((count, width), jnp.bfloat16),
            jax.ShapeDtypeStruct((BLK_DEV, CAP, width), jnp.bfloat16),
        ),
        compiler_params=params(),
        cost_estimate=pl.CostEstimate(flops=2 << 30, bytes_accessed=2 << 20, transcendentals=0),
        name="project",
    )(codes, queries, gain, weight)


def scatter_kernel(codes_ref, rows_ref, first_ref, middle_ref):
    rows = rows_ref[...]
    fill_slots(codes_ref, rows, first_ref, 0)
    fill_slots(codes_ref, rows, middle_ref, 1)


def scatter(codes, rows):
    shape = jax.ShapeDtypeStruct((BLK_DEV, CAP, rows.shape[1]), jnp.bfloat16)
    return pl.pallas_call(
        scatter_kernel,
        out_shape=(shape, shape),
        compiler_params=params(),
        cost_estimate=pl.CostEstimate(flops=3 << 30, bytes_accessed=2 << 20, transcendentals=0),
        name="scatter",
    )(codes, rows)


def attend_kernel(rows_ref, *refs, stack):
    kv_refs, out_ref = refs[:-1], refs[-1]
    blocks, count, width = rows_ref.shape
    head_size = width // HEADS
    factor = head_size ** (-0.5) * LOG2_E
    head_of = lax.broadcasted_iota(jnp.int32, (1, width), 1) // head_size
    pairs = [(kv_ref, i) for kv_ref in kv_refs for i in range(kv_ref.shape[0])]
    units = [(b, h) for b in range(blocks) for h in range(0, HEADS, stack)]

    def scores_of(unit):
        b, first = unit
        rows = rows_ref[b]
        kept = [jnp.where(head_of == first + i, rows, jnp.zeros_like(rows)) for i in range(stack)]
        kv_ref, i = pairs[b]
        return lax.dot_general(
            jnp.concatenate(kept, axis=0), kv_ref[i, :, :width],
            (((1,), (1,)), ((), ())), preferred_element_type=jnp.float32)

    scores = scores_of(units[0])
    merged = None
    for at, (b, first) in enumerate(units):
        following = scores_of(units[at + 1]) if at + 1 < len(units) else None
        peak = jnp.max(scores, axis=1, keepdims=True)
        expo = jnp.exp2((scores - peak) * factor)
        weights = (expo * (1.0 / jnp.sum(expo, axis=1, keepdims=True))).astype(jnp.bfloat16)
        kv_ref, i = pairs[b]
        got = jnp.dot(weights, kv_ref[i, :, width:], preferred_element_type=jnp.float32)
        for i in range(stack):
            part = got[i * count:(i + 1) * count]
            merged = part if first + i == 0 else jnp.where(head_of == first + i, part, merged)
        if first + stack == HEADS:
            out_ref[b] = merged.astype(jnp.bfloat16)
        scores = following


def attend(rows, kvs, part, blocks, name):
    _, count, width = rows.shape
    keys = kvs[0].shape[1]
    per_step = min(blocks, 4)
    steps = blocks // per_step
    if steps == 1:
        kv_specs = [whole(kv.shape) for kv in kvs]
    else:
        kv_specs = [pl.BlockSpec((per_step, keys, 2 * width), lambda g: (g, 0, 0))]
    pairs = blocks * count * keys
    return pl.pallas_call(
        functools.partial(attend_kernel, stack=2),
        grid=(steps,),
        in_specs=[pl.BlockSpec((per_step, count, width), lambda g: (g + part * steps, 0, 0))] + kv_specs,
        out_specs=pl.BlockSpec((per_step, count, width), lambda g: (g, 0, 0)),
        out_shape=jax.ShapeDtypeStruct((blocks, count, width), jnp.bfloat16),
        compiler_params=params(),
        cost_estimate=pl.CostEstimate(
            flops=4 * pairs * width * HEADS, bytes_accessed=blocks * keys * width * 4,
            transcendentals=pairs * HEADS),
        name=name,
    )(rows, *kvs)


def gathered(codes_ref, result_refs, at):
    entries = codes_ref.shape[1]
    count = at.shape[0]
    total = None
    for base, ref in result_refs:
        slots = ref.shape[0] * ref.shape[1]
        slot = lax.broadcasted_iota(jnp.int32, (count, slots), 1) + base
        hit = slot == at[:, 0:1]
        for entry in range(1, 3):
            hit = hit | (slot == at[:, entry:entry + 1])
        pick = jnp.where(hit, 1.0, 0.0).astype(jnp.bfloat16)
        got = jnp.dot(pick, ref[...].reshape(slots, ref.shape[2]), preferred_element_type=jnp.float32)
        total = got if total is None else total + got
    return total


def columns_of(codes_ref):
    entries, count = codes_ref.shape
    spare = jnp.full((8 - entries, count), -1, jnp.int32)
    return jnp.concatenate([codes_ref[...], spare], axis=0).T


def partial_kernel(codes_ref, *refs, bases):
    out_ref = refs[-1]
    at = columns_of(codes_ref)
    tile = 256
    for step in range(out_ref.shape[0] // tile):
        rows = slice(step * tile, (step + 1) * tile)
        out_ref[rows] = gathered(codes_ref, list(zip(bases, refs[:-1])), at[rows])


def partial_sum(codes, results, bases):
    width = results[0].shape[2]
    return pl.pallas_call(
        functools.partial(partial_kernel, bases=bases),
        out_shape=jax.ShapeDtypeStruct((codes.shape[1], width), jnp.float32),
        compiler_params=params(),
        cost_estimate=pl.CostEstimate(flops=3 << 30, bytes_accessed=2 << 20, transcendentals=0),
        name="partial_sum",
    )(codes, *results)


def final_kernel(codes_ref, partial_ref, queries_ref, weight_ref, *refs, bases):
    out_ref = refs[-1]
    at = columns_of(codes_ref)
    tile = 256
    for step in range(out_ref.shape[0] // tile):
        rows = slice(step * tile, (step + 1) * tile)
        total = partial_ref[rows] + gathered(codes_ref, list(zip(bases, refs[:-1])), at[rows])
        final = jnp.dot(total.astype(jnp.bfloat16), weight_ref[...], preferred_element_type=jnp.float32)
        out_ref[rows] = (final + queries_ref[rows].astype(jnp.float32)).astype(jnp.bfloat16)


def finish(codes, partial, queries, weight, results, bases):
    return pl.pallas_call(
        functools.partial(final_kernel, bases=bases),
        out_shape=jax.ShapeDtypeStruct(queries.shape, jnp.bfloat16),
        compiler_params=params(),
        cost_estimate=pl.CostEstimate(flops=1 << 30, bytes_accessed=2 << 20, transcendentals=0),
        name="finish",
    )(codes, partial, queries, weight, *results)


def shards(queries, norm_gain, w_query, w_key, w_value, w_out, features, visible, live):
    azim_cells, range_cells, width = queries.shape
    entries = visible.shape[2]
    count = azim_cells * range_cells
    bands = lax.axis_size("band")
    local_rows = features.shape[0]
    keys = bands * local_rows // BLK_DEV
    staged = bands == 4 and local_rows == 2 * keys

    shift = (lax.axis_index("band") * local_rows // keys) * CAP
    codes = jnp.where(live != 0, visible ^ shift, -1).transpose(2, 0, 1).reshape(entries, count)
    rows_in = queries.reshape(count, width)
    w_both = jnp.concatenate([w_key, w_value], axis=1)

    def keys_and_values(rows):
        both = jnp.dot(rows, w_both, preferred_element_type=jnp.float32).astype(jnp.bfloat16)
        return both.reshape(-1, keys, 2 * width)

    if staged:
        across = swapped(features, "band", 2)
        beside = swapped(features, "band", 1)
        beyond = swapped(across, "band", 1)
        parts = [[features, beside], [across, beyond]]
    else:
        held = features
        bit = 1
        while bit < bands:
            held = jnp.concatenate([held, swapped(held, "band", bit)], axis=0)
            bit *= 2
        parts = [[held]]
    blocks = BLK_DEV // len(parts)

    projected, slots_next = project(codes, rows_in, norm_gain.reshape(1, width), w_query)
    from_lower = shifted(slots_next, "sector", 1)
    slots_prev, slots_own = scatter(codes, projected)
    from_upper = shifted(slots_prev, "sector", -1)

    kvs = [[keys_and_values(rows) for rows in part] for part in parts]
    own = [attend(slots_own, kv, i, blocks, "own%d" % i) for i, kv in enumerate(kvs)]
    lower = [shifted(attend(from_lower, kv, i, blocks, "lower%d" % i), "sector", -1) for i, kv in enumerate(kvs)]
    upper = [shifted(attend(from_upper, kv, i, blocks, "upper%d" % i), "sector", 1) for i, kv in enumerate(kvs)]

    def bases(group):
        return tuple((group * BLK_DEV + i * blocks) * CAP for i in range(len(kvs)))

    partial = partial_sum(codes, own + lower, bases(1) + bases(2))
    out = finish(codes, partial, rows_in, w_out, upper, bases(0))
    return out.reshape(azim_cells, range_cells, width)


def solution(mesh):
    return jax.shard_map(
        shards,
        mesh=mesh,
        in_specs=(
            P("sector", "band", None),
            P(),
            P(),
            P(),
            P(),
            P(),
            P(("sector", "band"), None),
            P("sector", "band", None),
            P("sector", "band", None),
        ),
        out_specs=P("sector", "band", None),
        check_vma=False,
    )
```

```python
import functools

import jax
import jax.numpy as jnp
from jax import lax
from jax.experimental import pallas as pl
from jax.experimental.pallas import tpu as pltpu
from jax.sharding import PartitionSpec as P

HEADS = 8
BLK_DEV = 8
CAP = 128
LOG2_E = 1.4426950408889634
VMEM_BYTES = 24 << 20
UNROLL = 2


def params():
    return pltpu.CompilerParams(vmem_limit_bytes=VMEM_BYTES)


def shifted(block, axis, distance):
    count = lax.axis_size(axis)
    return lax.ppermute(block, axis, [(i, (i + distance) % count) for i in range(count)])


def swapped(block, axis, bit):
    count = lax.axis_size(axis)
    return lax.ppermute(block, axis, [(i, i ^ bit) for i in range(count)])


def fill_slots(codes_ref, rows, out_refs, group):
    blocks = out_refs[0].shape[0]
    queries = rows.shape[0]
    for step in range(0, BLK_DEV, 2):
        slot = lax.broadcasted_iota(jnp.int32, (2 * CAP, queries), 0) + (group * BLK_DEV + step) * CAP
        hit = slot == codes_ref[0:1, :]
        for entry in range(1, codes_ref.shape[0]):
            hit = hit | (slot == codes_ref[entry:entry + 1, :])
        pick = jnp.where(hit, 1.0, 0.0).astype(jnp.bfloat16)
        got = jnp.dot(pick, rows, preferred_element_type=jnp.float32).astype(jnp.bfloat16)
        at = step % blocks
        out_refs[step // blocks][at:at + 2] = got.reshape(2, CAP, got.shape[1])


def project_kernel(codes_ref, queries_ref, gain_ref, weight_ref, rows_ref, *slot_refs):
    values = queries_ref[...].astype(jnp.float32)
    average = jnp.mean(values, axis=-1, keepdims=True)
    centred = values - average
    spread = jnp.mean(centred * centred, axis=-1, keepdims=True)
    normed = (centred * lax.rsqrt(spread + 1e-05) * gain_ref[...]).astype(jnp.bfloat16)
    rows = jnp.dot(normed, weight_ref[...], preferred_element_type=jnp.float32).astype(jnp.bfloat16)
    rows_ref[...] = rows
    parts = len(slot_refs) // 2
    fill_slots(codes_ref, rows, slot_refs[:parts], 2)
    fill_slots(codes_ref, rows, slot_refs[parts:], 0)


def slot_shapes(parts, width):
    return (jax.ShapeDtypeStruct((BLK_DEV // parts, CAP, width), jnp.bfloat16),) * parts


def project(codes, queries, gain, weight, parts):
    count, width = queries.shape
    return pl.pallas_call(
        project_kernel,
        out_shape=(jax.ShapeDtypeStruct((count, width), jnp.bfloat16),) + 2 * slot_shapes(parts, width),
        compiler_params=params(),
        cost_estimate=pl.CostEstimate(flops=4 << 30, bytes_accessed=2 << 20, transcendentals=0),
        name="project",
    )(codes, queries, gain, weight)


def scatter_kernel(codes_ref, rows_ref, *slot_refs):
    fill_slots(codes_ref, rows_ref[...], slot_refs, 1)


def scatter(codes, rows, parts):
    return pl.pallas_call(
        scatter_kernel,
        out_shape=slot_shapes(parts, rows.shape[1]),
        compiler_params=params(),
        cost_estimate=pl.CostEstimate(flops=1 << 30, bytes_accessed=2 << 20, transcendentals=0),
        name="scatter",
    )(codes, rows)


def kv_kernel(key_ref, value_ref, *refs):
    out_ref = refs[-1]
    keys, width = out_ref.shape[1], key_ref.shape[1]
    done = 0
    for ref in refs[:-1]:
        for at in range(0, ref.shape[0], keys):
            rows = ref[at:at + keys]
            for side, weight_ref in enumerate((key_ref, value_ref)):
                got = jnp.dot(rows, weight_ref[...], preferred_element_type=jnp.float32)
                out_ref[done, :, side * width:(side + 1) * width] = got.astype(jnp.bfloat16)
            done += 1


def keys_and_values(features, w_key, w_value, keys):
    width = w_key.shape[1]
    count = sum(part.shape[0] for part in features)
    return pl.pallas_call(
        kv_kernel,
        out_shape=jax.ShapeDtypeStruct((count // keys, keys, 2 * width), jnp.bfloat16),
        compiler_params=params(),
        cost_estimate=pl.CostEstimate(flops=4 * count * width * width, bytes_accessed=6 * count * width, transcendentals=0),
        name="keys_and_values",
    )(w_key, w_value, *features)


def attend_kernel(rows_ref, kv_ref, out_ref, scores_ref, *, stack):
    blocks, count, width = rows_ref.shape
    head_size = width // HEADS
    factor = head_size ** (-0.5) * LOG2_E
    head_of = lax.broadcasted_iota(jnp.int32, (1, width), 1) // head_size
    firsts = list(range(0, HEADS, stack))

    def scores_of(b, first):
        rows = rows_ref[b]
        kept = [jnp.where(head_of == first + i, rows, jnp.zeros_like(rows)) for i in range(stack)]
        return lax.dot_general(
            jnp.concatenate(kept, axis=0), kv_ref[b, :, :width],
            (((1,), (1,)), ((), ())), preferred_element_type=jnp.float32)

    scores_ref[...] = scores_of(0, 0)

    @pl.loop(0, blocks // UNROLL)
    def _(step):
        scores = scores_ref[...]
        for unit in range(UNROLL):
            b = step * UNROLL + unit
            merged = None
            for at, first in enumerate(firsts):
                if at + 1 < len(firsts):
                    following = scores_of(b, firsts[at + 1])
                else:
                    following = scores_of(jnp.minimum(b + 1, blocks - 1), 0)
                peak = jnp.max(scores, axis=1, keepdims=True)
                expo = jnp.exp2((scores - peak) * factor)
                weights = (expo * (1.0 / jnp.sum(expo, axis=1, keepdims=True))).astype(jnp.bfloat16)
                got = jnp.dot(weights, kv_ref[b, :, width:], preferred_element_type=jnp.float32)
                for i in range(stack):
                    part = got[i * count:(i + 1) * count]
                    merged = part if first + i == 0 else jnp.where(head_of == first + i, part, merged)
                scores = following
            out_ref[b] = merged.astype(jnp.bfloat16)
        scores_ref[...] = scores


def attend(rows, kv, name):
    blocks, count, width = rows.shape
    keys = kv.shape[1]
    stack = 2
    pairs = blocks * count * keys
    return pl.pallas_call(
        functools.partial(attend_kernel, stack=stack),
        out_shape=jax.ShapeDtypeStruct(rows.shape, jnp.bfloat16),
        scratch_shapes=[pltpu.VMEM((stack * count, keys), jnp.float32)],
        compiler_params=params(),
        cost_estimate=pl.CostEstimate(
            flops=4 * pairs * width * HEADS, bytes_accessed=blocks * keys * width * 4,
            transcendentals=pairs * HEADS),
        name=name,
    )(rows, kv)


def gathered(codes_ref, result_refs, at):
    entries = codes_ref.shape[1]
    count = at.shape[0]
    total = None
    for base, ref in result_refs:
        slots = ref.shape[0] * ref.shape[1]
        slot = lax.broadcasted_iota(jnp.int32, (count, slots), 1) + base
        hit = slot == at[:, 0:1]
        for entry in range(1, 3):
            hit = hit | (slot == at[:, entry:entry + 1])
        pick = jnp.where(hit, 1.0, 0.0).astype(jnp.bfloat16)
        got = jnp.dot(pick, ref[...].reshape(slots, ref.shape[2]), preferred_element_type=jnp.float32)
        total = got if total is None else total + got
    return total


def columns_of(codes_ref):
    entries, count = codes_ref.shape
    spare = jnp.full((8 - entries, count), -1, jnp.int32)
    return jnp.concatenate([codes_ref[...], spare], axis=0).T


def partial_kernel(codes_ref, *refs, bases):
    out_ref = refs[-1]
    at = columns_of(codes_ref)
    tile = 256
    for step in range(out_ref.shape[0] // tile):
        rows = slice(step * tile, (step + 1) * tile)
        out_ref[rows] = gathered(codes_ref, list(zip(bases, refs[:-1])), at[rows])


def partial_sum(codes, results, bases):
    width = results[0].shape[2]
    return pl.pallas_call(
        functools.partial(partial_kernel, bases=bases),
        out_shape=jax.ShapeDtypeStruct((codes.shape[1], width), jnp.float32),
        compiler_params=params(),
        cost_estimate=pl.CostEstimate(flops=3 << 30, bytes_accessed=2 << 20, transcendentals=0),
        name="partial_sum",
    )(codes, *results)


def final_kernel(codes_ref, partial_ref, queries_ref, weight_ref, *refs, bases):
    out_ref = refs[-1]
    at = columns_of(codes_ref)
    tile = 256
    for step in range(out_ref.shape[0] // tile):
        rows = slice(step * tile, (step + 1) * tile)
        total = partial_ref[rows] + gathered(codes_ref, list(zip(bases, refs[:-1])), at[rows])
        final = jnp.dot(total.astype(jnp.bfloat16), weight_ref[...], preferred_element_type=jnp.float32)
        out_ref[rows] = (final + queries_ref[rows].astype(jnp.float32)).astype(jnp.bfloat16)


def finish(codes, partial, queries, weight, results, bases):
    return pl.pallas_call(
        functools.partial(final_kernel, bases=bases),
        out_shape=jax.ShapeDtypeStruct(queries.shape, jnp.bfloat16),
        compiler_params=params(),
        cost_estimate=pl.CostEstimate(flops=1 << 30, bytes_accessed=2 << 20, transcendentals=0),
        name="finish",
    )(codes, partial, queries, weight, *results)


def shards(queries, norm_gain, w_query, w_key, w_value, w_out, features, visible, live):
    azim_cells, range_cells, width = queries.shape
    entries = visible.shape[2]
    count = azim_cells * range_cells
    bands = lax.axis_size("band")
    local_rows = features.shape[0]
    keys = bands * local_rows // BLK_DEV
    staged = bands == 4 and local_rows == 2 * keys

    shift = (lax.axis_index("band") * local_rows // keys) * CAP
    codes = jnp.where(live != 0, visible ^ shift, -1).transpose(2, 0, 1).reshape(entries, count)
    rows_in = queries.reshape(count, width)

    if staged:
        across = swapped(features, "band", 2)
        held = [[features, swapped(features, "band", 1)]]
    else:
        whole_sector = features
        bit = 1
        while bit < bands:
            whole_sector = jnp.concatenate([whole_sector, swapped(whole_sector, "band", bit)], axis=0)
            bit *= 2
        held = [[whole_sector]]
    parts = 2 if staged else 1
    blocks = BLK_DEV // parts

    projected, *slots = project(codes, rows_in, norm_gain.reshape(1, width), w_query, parts)
    lower = [shifted(part, "sector", 1) for part in slots[:parts]]
    upper = [shifted(part, "sector", -1) for part in slots[parts:]]
    projected, *_ = lax.optimization_barrier((projected, *slots))
    own = list(scatter(codes, projected, parts))
    kv = keys_and_values(held[0], w_key, w_value, keys)
    own[0] = attend(own[0], kv, "own")

    if staged:
        across, own[0] = lax.optimization_barrier((across, own[0]))
        held.append([across, swapped(across, "band", 1)])

    def visit(part, kv, before):
        kv, first, second, before = lax.optimization_barrier((kv, lower[part], upper[part], before))
        first = attend(first, kv, "lower")
        second, first = lax.optimization_barrier((second, first))
        second = attend(second, kv, "upper")
        first, second = lax.optimization_barrier((first, second))
        return (shifted(first, "sector", -1), shifted(second, "sector", 1)), before, second

    sent, own[0], last = visit(0, kv, own[0])
    back = [sent]
    if staged:
        kv = keys_and_values(held[1], w_key, w_value, keys)
        sent, _, last = visit(1, kv, last)
        back.append(sent)
        own[1], _ = lax.optimization_barrier((own[1], last))
        own[1] = attend(own[1], kv, "own")

    def base(group, part):
        return (group * BLK_DEV + part * blocks) * CAP

    early = [(base(1, i), rows) for i, rows in enumerate(own)]
    early += [(base(2 - 2 * side, 0), back[0][side]) for side in range(2)] if staged else []
    late = [(base(2 - 2 * side, parts - 1), back[-1][side]) for side in range(2)]
    partial = partial_sum(codes, [rows for _, rows in early], tuple(at for at, _ in early))
    out = finish(codes, partial, rows_in, w_out, [rows for _, rows in late], tuple(at for at, _ in late))
    return out.reshape(azim_cells, range_cells, width)


def solution(mesh):
    return jax.shard_map(
        shards,
        mesh=mesh,
        in_specs=(
            P("sector", "band", None),
            P(),
            P(),
            P(),
            P(),
            P(),
            P(("sector", "band"), None),
            P("sector", "band", None),
            P("sector", "band", None),
        ),
        out_specs=P("sector", "band", None),
        check_vma=False,
    )
```

```python
import functools

import jax
import jax.numpy as jnp
from jax import lax
from jax.experimental import pallas as pl
from jax.experimental.pallas import tpu as pltpu
from jax.sharding import PartitionSpec as P


HEADS = 8
BLK_DEV = 8
CAP = 128
LOG2_E = 1.4426950408889634
VMEM_BYTES = 24 << 20
UNROLL = 2


def params():
    return pltpu.CompilerParams(vmem_limit_bytes=VMEM_BYTES)


def shifted(block, axis, distance):
    count = lax.axis_size(axis)
    return lax.ppermute(block, axis, [(i, (i + distance) % count) for i in range(count)])


def swapped(block, axis, bit):
    count = lax.axis_size(axis)
    return lax.ppermute(block, axis, [(i, i ^ bit) for i in range(count)])


def fill_slots(codes_ref, rows, out_refs, group):
    blocks = out_refs[0].shape[0]
    queries = rows.shape[0]
    codes = codes_ref[...]
    slot = lax.broadcasted_iota(jnp.int32, (2 * CAP, queries), 0).astype(jnp.int16)
    one, zero = jnp.ones((), jnp.bfloat16), jnp.zeros((), jnp.bfloat16)
    for step in range(0, BLK_DEV, 2):
        near = (codes - (group * BLK_DEV + step) * CAP).astype(jnp.int16)
        hit = slot == near[0:1, :]
        for entry in range(1, codes.shape[0]):
            hit = hit | (slot == near[entry:entry + 1, :])
        got = jnp.dot(jnp.where(hit, one, zero), rows, preferred_element_type=jnp.float32).astype(jnp.bfloat16)
        at = step % blocks
        out_refs[step // blocks][at:at + 2] = got.reshape(2, CAP, got.shape[1])


def project_kernel(codes_ref, queries_hbm, gain_hbm, weight_hbm, rows_ref, *refs):
    slot_refs, (queries_ref, gain_ref, weight_ref, sems) = refs[:-4], refs[-4:]
    copies = [
        pltpu.make_async_copy(source, target, sems.at[i])
        for i, (source, target) in enumerate(((queries_hbm, queries_ref), (gain_hbm, gain_ref), (weight_hbm, weight_ref)))
    ]
    for copy in copies:
        copy.start()
    for copy in copies:
        copy.wait()
    values = queries_ref[...].astype(jnp.float32)
    average = jnp.mean(values, axis=-1, keepdims=True)
    centred = values - average
    spread = jnp.mean(centred * centred, axis=-1, keepdims=True)
    normed = (centred * lax.rsqrt(spread + 1e-05) * gain_ref[...]).astype(jnp.bfloat16)
    rows = jnp.dot(normed, weight_ref[...], preferred_element_type=jnp.float32).astype(jnp.bfloat16)
    rows_ref[...] = rows
    parts = len(slot_refs) // 2
    fill_slots(codes_ref, rows, slot_refs[:parts], 2)
    fill_slots(codes_ref, rows, slot_refs[parts:], 0)


def slot_shapes(parts, width):
    return (jax.ShapeDtypeStruct((BLK_DEV // parts, CAP, width), jnp.bfloat16),) * parts


def project(codes, queries, gain, weight, parts):
    count, width = queries.shape
    hbm = pl.BlockSpec(memory_space=pltpu.HBM)
    return pl.pallas_call(
        project_kernel,
        in_specs=[pl.BlockSpec(memory_space=pltpu.VMEM), hbm, hbm, hbm],
        scratch_shapes=[
            pltpu.VMEM(queries.shape, queries.dtype),
            pltpu.VMEM(gain.shape, gain.dtype),
            pltpu.VMEM(weight.shape, weight.dtype),
            pltpu.SemaphoreType.DMA((3,)),
        ],
        out_shape=(jax.ShapeDtypeStruct((count, width), jnp.bfloat16),) + 2 * slot_shapes(parts, width),
        compiler_params=params(),
        cost_estimate=pl.CostEstimate(flops=4 << 30, bytes_accessed=2 << 20, transcendentals=0),
        name="project",
    )(codes, queries, gain, weight)


def scatter_kernel(codes_ref, rows_ref, *slot_refs):
    fill_slots(codes_ref, rows_ref[...], slot_refs, 1)


def scatter(codes, rows, parts):
    return pl.pallas_call(
        scatter_kernel,
        out_shape=slot_shapes(parts, rows.shape[1]),
        compiler_params=params(),
        cost_estimate=pl.CostEstimate(flops=1 << 30, bytes_accessed=2 << 20, transcendentals=0),
        name="scatter",
    )(codes, rows)


def kv_kernel(key_ref, value_ref, *refs):
    out_ref = refs[-1]
    keys, width = out_ref.shape[1], key_ref.shape[1]
    done = 0
    for ref in refs[:-1]:
        for at in range(0, ref.shape[0], keys):
            rows = ref[at:at + keys]
            for side, weight_ref in enumerate((key_ref, value_ref)):
                got = jnp.dot(rows, weight_ref[...], preferred_element_type=jnp.float32)
                out_ref[done, :, side * width:(side + 1) * width] = got.astype(jnp.bfloat16)
            done += 1


def keys_and_values(features, w_key, w_value, keys):
    width = w_key.shape[1]
    count = sum(part.shape[0] for part in features)
    return pl.pallas_call(
        kv_kernel,
        out_shape=jax.ShapeDtypeStruct((count // keys, keys, 2 * width), jnp.bfloat16),
        compiler_params=params(),
        cost_estimate=pl.CostEstimate(flops=4 * count * width * width, bytes_accessed=6 * count * width, transcendentals=0),
        name="keys_and_values",
    )(w_key, w_value, *features)


def attend_kernel(rows_ref, kv_ref, out_ref, scores_ref, *, stack):
    blocks, count, width = rows_ref.shape
    head_size = width // HEADS
    factor = head_size ** (-0.5) * LOG2_E
    head_of = lax.broadcasted_iota(jnp.int32, (1, width), 1) // head_size
    firsts = list(range(0, HEADS, stack))
    half = width // 2

    def scores_of(b, first):
        side = slice(half * (first >= HEADS // 2), half * (first >= HEADS // 2) + half)
        rows = rows_ref[b, :, side]
        kept = [jnp.where(head_of[:, side] == first + i, rows, jnp.zeros_like(rows)) for i in range(stack)]
        return lax.dot_general(
            jnp.concatenate(kept, axis=0), kv_ref[b, :, side],
            (((1,), (1,)), ((), ())), preferred_element_type=jnp.float32)

    scores_ref[...] = scores_of(0, 0)

    @pl.loop(0, blocks // UNROLL)
    def _(step):
        scores = scores_ref[...]
        for unit in range(UNROLL):
            b = step * UNROLL + unit
            merged = None
            for at, first in enumerate(firsts):
                if at + 1 < len(firsts):
                    following = scores_of(b, firsts[at + 1])
                else:
                    following = scores_of(jnp.minimum(b + 1, blocks - 1), 0)
                peak = jnp.max(scores, axis=1, keepdims=True)
                expo = jnp.exp2((scores - peak) * factor)
                weights = (expo * (1.0 / jnp.sum(expo, axis=1, keepdims=True))).astype(jnp.bfloat16)
                got = jnp.dot(weights, kv_ref[b, :, width:], preferred_element_type=jnp.float32)
                for i in range(stack):
                    part = got[i * count:(i + 1) * count]
                    merged = part if first + i == 0 else jnp.where(head_of == first + i, part, merged)
                scores = following
            out_ref[b] = merged.astype(jnp.bfloat16)
        scores_ref[...] = scores


def attend(rows, kv):
    blocks, count, width = rows.shape
    keys = kv.shape[1]
    stack = 2
    pairs = blocks * count * keys
    return pl.pallas_call(
        functools.partial(attend_kernel, stack=stack),
        out_shape=jax.ShapeDtypeStruct(rows.shape, jnp.bfloat16),
        scratch_shapes=[pltpu.VMEM((stack * count, keys), jnp.float32)],
        compiler_params=params(),
        cost_estimate=pl.CostEstimate(
            flops=4 * pairs * width * HEADS, bytes_accessed=blocks * keys * width * 4,
            transcendentals=pairs * HEADS),
    )(rows, kv)


def pick_kernel(codes_ref, *out_refs, groups):
    entries, count = codes_ref.shape
    spare = jnp.zeros((8 - entries, count), jnp.int32)
    at = jnp.concatenate([codes_ref[...], spare], axis=0).T
    lane = lax.broadcasted_iota(jnp.int32, (count, CAP), 1).astype(jnp.int16)
    near = [jnp.broadcast_to(at[:, entry:entry + 1], (count, CAP)).astype(jnp.int16) for entry in range(entries)]
    one, zero = jnp.ones((), jnp.bfloat16), jnp.zeros((), jnp.bfloat16)
    for group, out_ref in zip(groups, out_refs):
        for step in range(out_ref.shape[1] // CAP):
            slot = lane + jnp.int16(group * BLK_DEV * CAP + step * CAP)
            hit = slot == near[0]
            for entry in range(1, entries):
                hit = hit | (slot == near[entry])
            out_ref[:, step * CAP:(step + 1) * CAP] = jnp.where(hit, one, zero)


def picks(codes, groups):
    shape = jax.ShapeDtypeStruct((codes.shape[1], BLK_DEV * CAP), jnp.bfloat16)
    return pl.pallas_call(
        functools.partial(pick_kernel, groups=groups),
        out_shape=(shape,) * len(groups),
        compiler_params=params(),
        cost_estimate=pl.CostEstimate(flops=1 << 30, bytes_accessed=2 << 20, transcendentals=0),
        name="picks",
    )(codes)


def gathered(pick_refs, result_refs, places, rows):
    total = None
    for ref, (group, first) in zip(result_refs, places):
        slots = ref.shape[0] * ref.shape[1]
        got = jnp.dot(
            pick_refs[group][rows, first:first + slots], ref[...].reshape(slots, ref.shape[2]),
            preferred_element_type=jnp.float32)
        total = got if total is None else total + got
    return total


def partial_kernel(*refs, places):
    pick_refs, result_refs, out_ref = refs[:3], refs[3:-1], refs[-1]
    tile = 256
    for step in range(out_ref.shape[0] // tile):
        rows = slice(step * tile, (step + 1) * tile)
        out_ref[rows] = gathered(pick_refs, result_refs, places, rows)


def partial_sum(selected, results, places):
    return pl.pallas_call(
        functools.partial(partial_kernel, places=places),
        out_shape=jax.ShapeDtypeStruct((selected[0].shape[0], results[0].shape[2]), jnp.float32),
        compiler_params=params(),
        cost_estimate=pl.CostEstimate(flops=1 << 30, bytes_accessed=2 << 20, transcendentals=0),
        name="partial_sum",
    )(*selected, *results)


def final_kernel(partial_ref, queries_ref, weight_ref, *refs, places):
    pick_refs, result_refs, out_ref = refs[:3], refs[3:-1], refs[-1]
    tile = 256
    for step in range(out_ref.shape[0] // tile):
        rows = slice(step * tile, (step + 1) * tile)
        total = partial_ref[rows] + gathered(pick_refs, result_refs, places, rows)
        final = jnp.dot(total.astype(jnp.bfloat16), weight_ref[...], preferred_element_type=jnp.float32)
        out_ref[rows] = (final + queries_ref[rows].astype(jnp.float32)).astype(jnp.bfloat16)


def finish(partial, queries, weight, selected, results, places):
    return pl.pallas_call(
        functools.partial(final_kernel, places=places),
        out_shape=jax.ShapeDtypeStruct(queries.shape, jnp.bfloat16),
        compiler_params=params(),
        cost_estimate=pl.CostEstimate(flops=1 << 30, bytes_accessed=2 << 20, transcendentals=0),
        name="finish",
    )(partial, queries, weight, *selected, *results)


def shards(queries, norm_gain, w_query, w_key, w_value, w_out, features, visible, live):
    azim_cells, range_cells, width = queries.shape
    entries = visible.shape[2]
    count = azim_cells * range_cells
    bands = lax.axis_size("band")
    local_rows = features.shape[0]
    keys = bands * local_rows // BLK_DEV
    staged = bands == 4 and local_rows == 2 * keys

    shift = (lax.axis_index("band") * local_rows // keys) * CAP
    codes = jnp.where(live != 0, visible ^ shift, -1).transpose(2, 0, 1).reshape(entries, count)
    rows_in = queries.reshape(count, width)

    if staged:
        across = swapped(features, "band", 2)
        held = [[features, swapped(features, "band", 1)]]
    else:
        whole_sector = features
        bit = 1
        while bit < bands:
            whole_sector = jnp.concatenate([whole_sector, swapped(whole_sector, "band", bit)], axis=0)
            bit *= 2
        held = [[whole_sector]]
    parts = 2 if staged else 1
    blocks = BLK_DEV // parts

    projected, *slots = project(codes, rows_in, norm_gain.reshape(1, width), w_query, parts)
    lower, upper = [], []
    for part in range(parts):
        lower.append(shifted(slots[part], "sector", 1))
        upper.append(shifted(slots[parts + part], "sector", -1))
    projected, *_ = lax.optimization_barrier((projected, *slots))
    own = list(scatter(codes, projected, parts))
    kv = keys_and_values(held[0], w_key, w_value, keys)
    own[0] = attend(own[0], kv)
    codes, own[0] = lax.optimization_barrier((codes, own[0]))
    selected = picks(codes, (0, 1, 2))

    def visit(part, kv, before):
        kv, first, before = lax.optimization_barrier((kv, lower[part], before))
        second = upper[part]
        first = attend(first, kv)
        second, first = lax.optimization_barrier((second, first))
        middle = first
        second = attend(second, kv)
        first, second = lax.optimization_barrier((first, second))
        return (shifted(first, "sector", -1), shifted(second, "sector", 1)), before, middle, second

    sent, selected, middle, last = visit(0, kv, selected)
    back = [sent]
    if staged:
        across, middle = lax.optimization_barrier((across, middle))
        kv = keys_and_values([across, swapped(across, "band", 1)], w_key, w_value, keys)
        sent, _, _, last = visit(1, kv, last)
        back.append(sent)
        own[1], _ = lax.optimization_barrier((own[1], last))
        own[1] = attend(own[1], kv)

    slots_of = blocks * CAP
    early = [((1, i * slots_of), rows) for i, rows in enumerate(own)]
    early += [((2 - 2 * side, 0), back[0][side]) for side in range(2)] if staged else []
    late = [((2 - 2 * side, (parts - 1) * slots_of), back[-1][side]) for side in range(2)]
    partial = partial_sum(selected, [rows for _, rows in early], tuple(at for at, _ in early))
    out = finish(partial, rows_in, w_out, selected, [rows for _, rows in late], tuple(at for at, _ in late))
    return out.reshape(azim_cells, range_cells, width)


def solution(mesh):
    return jax.shard_map(
        shards,
        mesh=mesh,
        in_specs=(
            P("sector", "band", None),
            P(),
            P(),
            P(),
            P(),
            P(),
            P(("sector", "band"), None),
            P("sector", "band", None),
            P("sector", "band", None),
        ),
        out_specs=P("sector", "band", None),
        check_vma=False,
    )
```

```python
import functools

import jax
import jax.numpy as jnp
from jax import lax
from jax.experimental import pallas as pl
from jax.experimental.pallas import tpu as pltpu
from jax.sharding import PartitionSpec as P


HEADS = 8
BLK_DEV = 8
CAP = 128
LOG2_E = 1.4426950408889634
VMEM_BYTES = 24 << 20
UNROLL = 2


def params():
    return pltpu.CompilerParams(vmem_limit_bytes=VMEM_BYTES)


def shifted(block, axis, distance):
    count = lax.axis_size(axis)
    return lax.ppermute(block, axis, [(i, (i + distance) % count) for i in range(count)])


def swapped(block, axis, bit):
    count = lax.axis_size(axis)
    return lax.ppermute(block, axis, [(i, i ^ bit) for i in range(count)])


def fill_slots(codes_ref, rows, out_ref, group):
    queries = rows.shape[0]
    codes = codes_ref[...]
    slot = lax.broadcasted_iota(jnp.int32, (2 * CAP, queries), 0).astype(jnp.int16)
    one, zero = jnp.ones((), jnp.bfloat16), jnp.zeros((), jnp.bfloat16)
    for step in range(0, BLK_DEV, 2):
        near = (codes - (group * BLK_DEV + step) * CAP).astype(jnp.int16)
        hit = slot == near[0:1, :]
        for entry in range(1, codes.shape[0]):
            hit = hit | (slot == near[entry:entry + 1, :])
        got = jnp.dot(jnp.where(hit, one, zero), rows, preferred_element_type=jnp.float32).astype(jnp.bfloat16)
        out_ref[step:step + 2] = got.reshape(2, CAP, got.shape[1])


def project_kernel(codes_ref, queries_hbm, gain_hbm, weight_hbm, rows_ref, *refs):
    slots_ref, queries_ref, gain_ref, weight_ref, sems = refs
    copies = [
        pltpu.make_async_copy(source, target, sems.at[i])
        for i, (source, target) in enumerate(((queries_hbm, queries_ref), (gain_hbm, gain_ref), (weight_hbm, weight_ref)))
    ]
    for copy in copies:
        copy.start()
    for copy in copies:
        copy.wait()
    values = queries_ref[...].astype(jnp.float32)
    average = jnp.mean(values, axis=-1, keepdims=True)
    centred = values - average
    spread = jnp.mean(centred * centred, axis=-1, keepdims=True)
    normed = (centred * lax.rsqrt(spread + 1e-05) * gain_ref[...]).astype(jnp.bfloat16)
    rows = jnp.dot(normed, weight_ref[...], preferred_element_type=jnp.float32).astype(jnp.bfloat16)
    rows_ref[...] = rows
    fill_slots(codes_ref, rows, slots_ref, 2)


def slot_shape(width):
    return jax.ShapeDtypeStruct((BLK_DEV, CAP, width), jnp.bfloat16)


def project(codes, queries, gain, weight):
    count, width = queries.shape
    hbm = pl.BlockSpec(memory_space=pltpu.HBM)
    return pl.pallas_call(
        project_kernel,
        in_specs=[pl.BlockSpec(memory_space=pltpu.VMEM), hbm, hbm, hbm],
        scratch_shapes=[
            pltpu.VMEM(queries.shape, queries.dtype),
            pltpu.VMEM(gain.shape, gain.dtype),
            pltpu.VMEM(weight.shape, weight.dtype),
            pltpu.SemaphoreType.DMA((3,)),
        ],
        out_shape=(jax.ShapeDtypeStruct((count, width), jnp.bfloat16), slot_shape(width)),
        compiler_params=params(),
        cost_estimate=pl.CostEstimate(flops=4 << 30, bytes_accessed=2 << 20, transcendentals=0),
        name="project",
    )(codes, queries, gain, weight)


def scatter_kernel(codes_ref, rows_ref, prev_ref, own_ref):
    rows = rows_ref[...]
    fill_slots(codes_ref, rows, prev_ref, 0)
    fill_slots(codes_ref, rows, own_ref, 1)


def scatter(codes, rows):
    return pl.pallas_call(
        scatter_kernel,
        out_shape=(slot_shape(rows.shape[1]),) * 2,
        compiler_params=params(),
        cost_estimate=pl.CostEstimate(flops=1 << 30, bytes_accessed=2 << 20, transcendentals=0),
        name="scatter",
    )(codes, rows)


def kv_kernel(key_ref, value_ref, *refs):
    out_ref = refs[-1]
    keys, width = out_ref.shape[1], key_ref.shape[1]
    done = 0
    for ref in refs[:-1]:
        for at in range(0, ref.shape[0], keys):
            rows = ref[at:at + keys]
            for side, weight_ref in enumerate((key_ref, value_ref)):
                got = jnp.dot(rows, weight_ref[...], preferred_element_type=jnp.float32)
                out_ref[done, :, side * width:(side + 1) * width] = got.astype(jnp.bfloat16)
            done += 1


def keys_and_values(features, w_key, w_value, keys):
    width = w_key.shape[1]
    count = sum(part.shape[0] for part in features)
    return pl.pallas_call(
        kv_kernel,
        out_shape=jax.ShapeDtypeStruct((count // keys, keys, 2 * width), jnp.bfloat16),
        compiler_params=params(),
        cost_estimate=pl.CostEstimate(flops=4 * count * width * width, bytes_accessed=6 * count * width, transcendentals=0),
        name="keys_and_values",
    )(w_key, w_value, *features)


def attend_kernel(rows_ref, kv_ref, *refs, stack, start):
    out_ref, scores_ref = refs[-2:]
    blocks, (_, count, width) = kv_ref.shape[0], rows_ref.shape
    if len(refs) > 2:
        out_ref[:start] = refs[0][...]
    base = out_ref.shape[0] - blocks
    head_size = width // HEADS
    factor = head_size ** (-0.5) * LOG2_E
    head_of = lax.broadcasted_iota(jnp.int32, (1, width), 1) // head_size
    firsts = list(range(0, HEADS, stack))
    half = width // 2

    def scores_of(b, first):
        side = slice(half * (first >= HEADS // 2), half * (first >= HEADS // 2) + half)
        rows = rows_ref[start + b, :, side]
        kept = [jnp.where(head_of[:, side] == first + i, rows, jnp.zeros_like(rows)) for i in range(stack)]
        return lax.dot_general(
            jnp.concatenate(kept, axis=0), kv_ref[b, :, side],
            (((1,), (1,)), ((), ())), preferred_element_type=jnp.float32)

    scores_ref[...] = scores_of(0, 0)

    @pl.loop(0, blocks // UNROLL)
    def _(step):
        scores = scores_ref[...]
        for unit in range(UNROLL):
            b = step * UNROLL + unit
            merged = None
            for at, first in enumerate(firsts):
                if at + 1 < len(firsts):
                    following = scores_of(b, firsts[at + 1])
                else:
                    following = scores_of(jnp.minimum(b + 1, blocks - 1), 0)
                peak = jnp.max(scores, axis=1, keepdims=True)
                expo = jnp.exp2((scores - peak) * factor)
                weights = (expo * (1.0 / jnp.sum(expo, axis=1, keepdims=True))).astype(jnp.bfloat16)
                got = jnp.dot(weights, kv_ref[b, :, width:], preferred_element_type=jnp.float32)
                for i in range(stack):
                    part = got[i * count:(i + 1) * count]
                    merged = part if first + i == 0 else jnp.where(head_of == first + i, part, merged)
                scores = following
            out_ref[base + b] = merged.astype(jnp.bfloat16)
        scores_ref[...] = scores


def attend(rows, kv, start, before=None):
    _, count, width = rows.shape
    blocks, keys = kv.shape[:2]
    stack = 2
    pairs = blocks * count * keys
    done = 0 if before is None else start
    return pl.pallas_call(
        functools.partial(attend_kernel, stack=stack, start=start),
        out_shape=jax.ShapeDtypeStruct((done + blocks, count, width), jnp.bfloat16),
        scratch_shapes=[pltpu.VMEM((stack * count, keys), jnp.float32)],
        compiler_params=params(),
        cost_estimate=pl.CostEstimate(
            flops=4 * pairs * width * HEADS, bytes_accessed=blocks * keys * width * 4,
            transcendentals=pairs * HEADS),
        name="attend",
    )(rows, kv, *([] if before is None else [before]))


def pick_kernel(codes_ref, *out_refs, groups):
    entries, count = codes_ref.shape
    spare = jnp.zeros((8 - entries, count), jnp.int32)
    at = jnp.concatenate([codes_ref[...], spare], axis=0).T
    lane = lax.broadcasted_iota(jnp.int32, (count, CAP), 1).astype(jnp.int16)
    near = [jnp.broadcast_to(at[:, entry:entry + 1], (count, CAP)).astype(jnp.int16) for entry in range(entries)]
    one, zero = jnp.ones((), jnp.bfloat16), jnp.zeros((), jnp.bfloat16)
    for group, out_ref in zip(groups, out_refs):
        for step in range(out_ref.shape[1] // CAP):
            slot = lane + jnp.int16(group * BLK_DEV * CAP + step * CAP)
            hit = slot == near[0]
            for entry in range(1, entries):
                hit = hit | (slot == near[entry])
            out_ref[:, step * CAP:(step + 1) * CAP] = jnp.where(hit, one, zero)


def picks(codes, groups):
    shape = jax.ShapeDtypeStruct((codes.shape[1], BLK_DEV * CAP), jnp.bfloat16)
    return pl.pallas_call(
        functools.partial(pick_kernel, groups=groups),
        out_shape=(shape,) * len(groups),
        compiler_params=params(),
        cost_estimate=pl.CostEstimate(flops=1 << 30, bytes_accessed=2 << 20, transcendentals=0),
        name="picks",
    )(codes)


def gathered(pick_refs, result_refs, places, rows):
    total = None
    for ref, (group, first) in zip(result_refs, places):
        slots = ref.shape[0] * ref.shape[1]
        got = jnp.dot(
            pick_refs[group][rows, first:first + slots], ref[...].reshape(slots, ref.shape[2]),
            preferred_element_type=jnp.float32)
        total = got if total is None else total + got
    return total


def partial_kernel(*refs, places):
    pick_refs, result_refs, out_ref = refs[:3], refs[3:-1], refs[-1]
    tile = 256
    for step in range(out_ref.shape[0] // tile):
        rows = slice(step * tile, (step + 1) * tile)
        out_ref[rows] = gathered(pick_refs, result_refs, places, rows)


def partial_sum(selected, results, places):
    return pl.pallas_call(
        functools.partial(partial_kernel, places=places),
        out_shape=jax.ShapeDtypeStruct((selected[0].shape[0], results[0].shape[2]), jnp.float32),
        compiler_params=params(),
        cost_estimate=pl.CostEstimate(flops=1 << 30, bytes_accessed=2 << 20, transcendentals=0),
        name="partial_sum",
    )(*selected, *results)


def final_kernel(partial_ref, queries_ref, weight_ref, *refs, places):
    pick_refs, result_refs, out_ref = refs[:3], refs[3:-1], refs[-1]
    tile = 256
    for step in range(out_ref.shape[0] // tile):
        rows = slice(step * tile, (step + 1) * tile)
        total = partial_ref[rows] + gathered(pick_refs, result_refs, places, rows)
        final = jnp.dot(total.astype(jnp.bfloat16), weight_ref[...], preferred_element_type=jnp.float32)
        out_ref[rows] = (final + queries_ref[rows].astype(jnp.float32)).astype(jnp.bfloat16)


def finish(partial, queries, weight, selected, results, places):
    return pl.pallas_call(
        functools.partial(final_kernel, places=places),
        out_shape=jax.ShapeDtypeStruct(queries.shape, jnp.bfloat16),
        compiler_params=params(),
        cost_estimate=pl.CostEstimate(flops=1 << 30, bytes_accessed=2 << 20, transcendentals=0),
        name="finish",
    )(partial, queries, weight, *selected, *results)


def shards(queries, norm_gain, w_query, w_key, w_value, w_out, features, visible, live):
    azim_cells, range_cells, width = queries.shape
    entries = visible.shape[2]
    count = azim_cells * range_cells
    bands = lax.axis_size("band")
    local_rows = features.shape[0]
    keys = bands * local_rows // BLK_DEV
    staged = bands == 4 and local_rows == 2 * keys

    shift = (lax.axis_index("band") * local_rows // keys) * CAP
    codes = jnp.where(live != 0, visible ^ shift, -1).transpose(2, 0, 1).reshape(entries, count)
    rows_in = queries.reshape(count, width)

    if staged:
        across = swapped(features, "band", 2)
        held = [[features, swapped(features, "band", 1)]]
    else:
        whole_sector = features
        bit = 1
        while bit < bands:
            whole_sector = jnp.concatenate([whole_sector, swapped(whole_sector, "band", bit)], axis=0)
            bit *= 2
        held = [[whole_sector]]
    selected = picks(codes, (0, 1, 2))
    codes, *selected = lax.optimization_barrier((codes, *selected))
    projected, slots_next = project(codes, rows_in, norm_gain.reshape(1, width), w_query)
    lower = shifted(slots_next, "sector", 1)
    projected, _ = lax.optimization_barrier((projected, slots_next))
    slots_prev, slots_own = scatter(codes, projected)
    kv = keys_and_values(held[0], w_key, w_value, keys)
    half = kv.shape[0]
    own = [attend(slots_own, kv, 0)]
    slots_prev, own[0] = lax.optimization_barrier((slots_prev, own[0]))
    upper = shifted(slots_prev, "sector", -1)
    kv, lower, own[0] = lax.optimization_barrier((kv, lower, own[0]))
    from_lower = attend(lower, kv, 0)
    kvs = [kv]
    if staged:
        across, from_lower = lax.optimization_barrier((across, from_lower))
        kvs.append(keys_and_values([across, swapped(across, "band", 1)], w_key, w_value, keys))
        from_lower = attend(lower, kvs[1], half, from_lower)
    back_lower = shifted(from_lower, "sector", -1)
    back_upper = []
    last = from_lower
    for part, kv in enumerate(kvs):
        turn, last = lax.optimization_barrier((upper, last))
        last = attend(turn, kv, part * half)
        back_upper.append(shifted(last, "sector", 1))
    if staged:
        turn, last = lax.optimization_barrier((slots_own, last))
        own.append(attend(turn, kvs[1], half))

    cuts = [i * half * CAP for i in range(len(kvs))]
    early = [((1, at), rows) for at, rows in zip(cuts, own)] + [((2, 0), back_lower)]
    early += [((0, at), rows) for at, rows in zip(cuts[:-1], back_upper)]
    partial = partial_sum(selected, [rows for _, rows in early], tuple(at for at, _ in early))
    out = finish(partial, rows_in, w_out, selected, back_upper[-1:], ((0, cuts[-1]),))
    return out.reshape(azim_cells, range_cells, width)


def solution(mesh):
    return jax.shard_map(
        shards,
        mesh=mesh,
        in_specs=(
            P("sector", "band", None),
            P(),
            P(),
            P(),
            P(),
            P(),
            P(("sector", "band"), None),
            P("sector", "band", None),
            P("sector", "band", None),
        ),
        out_specs=P("sector", "band", None),
        check_vma=False,
    )
```

```python
import functools

import jax
import jax.numpy as jnp
from jax import lax
from jax.experimental import pallas as pl
from jax.experimental.pallas import tpu as pltpu
from jax.sharding import PartitionSpec as P


HEADS = 8
BLK_DEV = 8
CAP = 128
LOG2_E = 1.4426950408889634
VMEM_BYTES = 24 << 20
UNROLL = 2


def params():
    return pltpu.CompilerParams(vmem_limit_bytes=VMEM_BYTES)


def shifted(block, axis, distance):
    count = lax.axis_size(axis)
    return lax.ppermute(block, axis, [(i, (i + distance) % count) for i in range(count)])


def swapped(block, axis, bit):
    count = lax.axis_size(axis)
    return lax.ppermute(block, axis, [(i, i ^ bit) for i in range(count)])


def fill_slots(codes_ref, rows, out_ref, first):
    queries = rows.shape[0]
    codes = codes_ref[...]
    slot = lax.broadcasted_iota(jnp.int32, (2 * CAP, queries), 0).astype(jnp.int16)
    one, zero = jnp.ones((), jnp.bfloat16), jnp.zeros((), jnp.bfloat16)
    for step in range(0, out_ref.shape[0], 2):
        near = (codes - (first + step) * CAP).astype(jnp.int16)
        hit = slot == near[0:1, :]
        for entry in range(1, codes.shape[0]):
            hit = hit | (slot == near[entry:entry + 1, :])
        got = jnp.dot(jnp.where(hit, one, zero), rows, preferred_element_type=jnp.float32).astype(jnp.bfloat16)
        out_ref[step:step + 2] = got.reshape(2, CAP, got.shape[1])


def project_kernel(codes_ref, queries_hbm, gain_hbm, weight_hbm, rows_ref, *refs):
    lower_ref, upper_ref, queries_ref, gain_ref, weight_ref, sems = refs
    copies = [
        pltpu.make_async_copy(source, target, sems.at[i])
        for i, (source, target) in enumerate(((queries_hbm, queries_ref), (gain_hbm, gain_ref), (weight_hbm, weight_ref)))
    ]
    for copy in copies:
        copy.start()
    for copy in copies:
        copy.wait()
    values = queries_ref[...].astype(jnp.float32)
    average = jnp.mean(values, axis=-1, keepdims=True)
    centred = values - average
    spread = jnp.mean(centred * centred, axis=-1, keepdims=True)
    normed = (centred * lax.rsqrt(spread + 1e-05) * gain_ref[...]).astype(jnp.bfloat16)
    rows = jnp.dot(normed, weight_ref[...], preferred_element_type=jnp.float32).astype(jnp.bfloat16)
    rows_ref[...] = rows
    fill_slots(codes_ref, rows, lower_ref, 2 * BLK_DEV)
    fill_slots(codes_ref, rows, upper_ref, 0)


def slot_shape(blocks, width):
    return jax.ShapeDtypeStruct((blocks, CAP, width), jnp.bfloat16)


def project(codes, queries, gain, weight, blocks):
    count, width = queries.shape
    hbm = pl.BlockSpec(memory_space=pltpu.HBM)
    return pl.pallas_call(
        project_kernel,
        in_specs=[pl.BlockSpec(memory_space=pltpu.VMEM), hbm, hbm, hbm],
        scratch_shapes=[
            pltpu.VMEM(queries.shape, queries.dtype),
            pltpu.VMEM(gain.shape, gain.dtype),
            pltpu.VMEM(weight.shape, weight.dtype),
            pltpu.SemaphoreType.DMA((3,)),
        ],
        out_shape=(jax.ShapeDtypeStruct((count, width), jnp.bfloat16),) + (slot_shape(blocks, width),) * 2,
        compiler_params=params(),
        cost_estimate=pl.CostEstimate(flops=4 << 30, bytes_accessed=2 << 20, transcendentals=0),
        name="project",
    )(codes, queries, gain, weight)


def scatter_kernel(codes_ref, rows_ref, own_ref, *refs, blocks):
    rows = rows_ref[...]
    for ref, first in zip(refs, (2 * BLK_DEV + blocks, blocks)):
        fill_slots(codes_ref, rows, ref, first)
    fill_slots(codes_ref, rows, own_ref, BLK_DEV)


def scatter(codes, rows, blocks):
    width = rows.shape[1]
    rest = BLK_DEV - blocks
    return pl.pallas_call(
        functools.partial(scatter_kernel, blocks=blocks),
        out_shape=(slot_shape(BLK_DEV, width),) + ((slot_shape(rest, width),) * 2 if rest else ()),
        compiler_params=params(),
        cost_estimate=pl.CostEstimate(flops=1 << 30, bytes_accessed=2 << 20, transcendentals=0),
        name="scatter",
    )(codes, rows)


def kv_kernel(key_ref, value_ref, *refs):
    out_ref = refs[-1]
    keys, width = out_ref.shape[1], key_ref.shape[1]
    done = 0
    for ref in refs[:-1]:
        for at in range(0, ref.shape[0], keys):
            rows = ref[at:at + keys]
            for side, weight_ref in enumerate((key_ref, value_ref)):
                got = jnp.dot(rows, weight_ref[...], preferred_element_type=jnp.float32)
                out_ref[done, :, side * width:(side + 1) * width] = got.astype(jnp.bfloat16)
            done += 1


def keys_and_values(features, w_key, w_value, keys):
    width = w_key.shape[1]
    count = sum(part.shape[0] for part in features)
    return pl.pallas_call(
        kv_kernel,
        out_shape=jax.ShapeDtypeStruct((count // keys, keys, 2 * width), jnp.bfloat16),
        compiler_params=params(),
        cost_estimate=pl.CostEstimate(flops=4 * count * width * width, bytes_accessed=6 * count * width, transcendentals=0),
        name="keys_and_values",
    )(w_key, w_value, *features)


def attend_kernel(rows_ref, kv_ref, out_ref, scores_ref, *, stack, start):
    blocks, (_, count, width) = kv_ref.shape[0], rows_ref.shape
    head_size = width // HEADS
    factor = head_size ** (-0.5) * LOG2_E
    head_of = lax.broadcasted_iota(jnp.int32, (1, width), 1) // head_size
    firsts = list(range(0, HEADS, stack))
    half = width // 2

    def scores_of(b, first):
        side = slice(half * (first >= HEADS // 2), half * (first >= HEADS // 2) + half)
        rows = rows_ref[start + b, :, side]
        kept = [jnp.where(head_of[:, side] == first + i, rows, jnp.zeros_like(rows)) for i in range(stack)]
        return lax.dot_general(
            jnp.concatenate(kept, axis=0), kv_ref[b, :, side],
            (((1,), (1,)), ((), ())), preferred_element_type=jnp.float32)

    scores_ref[...] = scores_of(0, 0)

    @pl.loop(0, blocks // UNROLL)
    def _(step):
        scores = scores_ref[...]
        for unit in range(UNROLL):
            b = step * UNROLL + unit
            merged = None
            for at, first in enumerate(firsts):
                if at + 1 < len(firsts):
                    following = scores_of(b, firsts[at + 1])
                else:
                    following = scores_of(jnp.minimum(b + 1, blocks - 1), 0)
                peak = jnp.max(scores, axis=1, keepdims=True)
                expo = jnp.exp2((scores - peak) * factor)
                weights = (expo * (1.0 / jnp.sum(expo, axis=1, keepdims=True))).astype(jnp.bfloat16)
                got = jnp.dot(weights, kv_ref[b, :, width:], preferred_element_type=jnp.float32)
                for i in range(stack):
                    part = got[i * count:(i + 1) * count]
                    merged = part if first + i == 0 else jnp.where(head_of == first + i, part, merged)
                scores = following
            out_ref[b] = merged.astype(jnp.bfloat16)
        scores_ref[...] = scores


def attend(rows, kv, start=0):
    _, count, width = rows.shape
    blocks, keys = kv.shape[:2]
    stack = 2
    pairs = blocks * count * keys
    return pl.pallas_call(
        functools.partial(attend_kernel, stack=stack, start=start),
        out_shape=jax.ShapeDtypeStruct((blocks, count, width), jnp.bfloat16),
        scratch_shapes=[pltpu.VMEM((stack * count, keys), jnp.float32)],
        compiler_params=params(),
        cost_estimate=pl.CostEstimate(
            flops=4 * pairs * width * HEADS, bytes_accessed=blocks * keys * width * 4,
            transcendentals=pairs * HEADS),
        name="attend",
    )(rows, kv)


def pick_kernel(codes_ref, *out_refs, groups):
    entries, count = codes_ref.shape
    spare = jnp.zeros((8 - entries, count), jnp.int32)
    at = jnp.concatenate([codes_ref[...], spare], axis=0).T
    lane = lax.broadcasted_iota(jnp.int32, (count, CAP), 1).astype(jnp.int16)
    near = [jnp.broadcast_to(at[:, entry:entry + 1], (count, CAP)).astype(jnp.int16) for entry in range(entries)]
    one, zero = jnp.ones((), jnp.bfloat16), jnp.zeros((), jnp.bfloat16)
    for group, out_ref in zip(groups, out_refs):
        for step in range(out_ref.shape[1] // CAP):
            slot = lane + jnp.int16(group * BLK_DEV * CAP + step * CAP)
            hit = slot == near[0]
            for entry in range(1, entries):
                hit = hit | (slot == near[entry])
            out_ref[:, step * CAP:(step + 1) * CAP] = jnp.where(hit, one, zero)


def picks(codes, groups):
    shape = jax.ShapeDtypeStruct((codes.shape[1], BLK_DEV * CAP), jnp.bfloat16)
    return pl.pallas_call(
        functools.partial(pick_kernel, groups=groups),
        out_shape=(shape,) * len(groups),
        compiler_params=params(),
        cost_estimate=pl.CostEstimate(flops=1 << 30, bytes_accessed=2 << 20, transcendentals=0),
        name="picks",
    )(codes)


def gathered(pick_refs, result_refs, places, rows):
    total = None
    for ref, (group, first) in zip(result_refs, places):
        slots = ref.shape[0] * ref.shape[1]
        got = jnp.dot(
            pick_refs[group][rows, first:first + slots], ref[...].reshape(slots, ref.shape[2]),
            preferred_element_type=jnp.float32)
        total = got if total is None else total + got
    return total


def partial_kernel(*refs, places):
    pick_refs, result_refs, out_ref = refs[:3], refs[3:-1], refs[-1]
    tile = 256
    for step in range(out_ref.shape[0] // tile):
        rows = slice(step * tile, (step + 1) * tile)
        out_ref[rows] = gathered(pick_refs, result_refs, places, rows)


def partial_sum(selected, results, places):
    return pl.pallas_call(
        functools.partial(partial_kernel, places=places),
        out_shape=jax.ShapeDtypeStruct((selected[0].shape[0], results[0].shape[2]), jnp.float32),
        compiler_params=params(),
        cost_estimate=pl.CostEstimate(flops=1 << 30, bytes_accessed=2 << 20, transcendentals=0),
        name="partial_sum",
    )(*selected, *results)


def final_kernel(partial_ref, queries_ref, weight_ref, *refs, places):
    pick_refs, result_refs, out_ref = refs[:3], refs[3:-1], refs[-1]
    tile = 256
    for step in range(out_ref.shape[0] // tile):
        rows = slice(step * tile, (step + 1) * tile)
        total = partial_ref[rows] + gathered(pick_refs, result_refs, places, rows)
        final = jnp.dot(total.astype(jnp.bfloat16), weight_ref[...], preferred_element_type=jnp.float32)
        out_ref[rows] = (final + queries_ref[rows].astype(jnp.float32)).astype(jnp.bfloat16)


def finish(partial, queries, weight, selected, results, places):
    return pl.pallas_call(
        functools.partial(final_kernel, places=places),
        out_shape=jax.ShapeDtypeStruct(queries.shape, jnp.bfloat16),
        compiler_params=params(),
        cost_estimate=pl.CostEstimate(flops=1 << 30, bytes_accessed=2 << 20, transcendentals=0),
        name="finish",
    )(partial, queries, weight, *selected, *results)


def shards(queries, norm_gain, w_query, w_key, w_value, w_out, features, visible, live):
    azim_cells, range_cells, width = queries.shape
    entries = visible.shape[2]
    count = azim_cells * range_cells
    bands = lax.axis_size("band")
    local_rows = features.shape[0]
    keys = bands * local_rows // BLK_DEV
    staged = bands == 4 and local_rows == 2 * keys

    shift = (lax.axis_index("band") * local_rows // keys) * CAP
    codes = jnp.where(live != 0, visible ^ shift, -1).transpose(2, 0, 1).reshape(entries, count)
    rows_in = queries.reshape(count, width)

    if staged:
        across = swapped(features, "band", 2)
        held = [[features, swapped(features, "band", 1)]]
    else:
        whole_sector = features
        bit = 1
        while bit < bands:
            whole_sector = jnp.concatenate([whole_sector, swapped(whole_sector, "band", bit)], axis=0)
            bit *= 2
        held = [[whole_sector]]
    selected = picks(codes, (0, 1, 2))
    codes, *selected = lax.optimization_barrier((codes, *selected))
    blocks = BLK_DEV // 2 if staged else BLK_DEV
    projected, *ready = project(codes, rows_in, norm_gain.reshape(1, width), w_query, blocks)

    def send(lower, upper):
        lower = shifted(lower, "sector", 1)
        return lower, shifted(upper, "sector", -1)

    visits = [send(*ready)]
    projected, *_ = lax.optimization_barrier((projected, *ready))
    slots_own, *ready = scatter(codes, projected, blocks)
    kvs = [keys_and_values(held[0], w_key, w_value, keys)]
    own = [attend(slots_own, kvs[0])]
    last = own[0]
    if staged:
        *ready, last = lax.optimization_barrier((*ready, last))
        visits.append(send(*ready))
    back = []
    for part, (lower, upper) in enumerate(visits):
        if part:
            kvs.append(keys_and_values([across, beyond], w_key, w_value, keys))
        lower, last = lax.optimization_barrier((lower, last))
        lower = attend(lower, kvs[part])
        if staged and not part:
            across, lower = lax.optimization_barrier((across, lower))
            beyond = swapped(across, "band", 1)
        upper, lower = lax.optimization_barrier((upper, lower))
        upper = attend(upper, kvs[part])
        lower, upper = lax.optimization_barrier((lower, upper))
        back.append((shifted(lower, "sector", -1), shifted(upper, "sector", 1)))
        last = upper
    if staged:
        turn, last = lax.optimization_barrier((slots_own, last))
        own.append(attend(turn, kvs[1], blocks))

    cuts = [i * blocks * CAP for i in range(len(kvs))]
    early = [((1, at), rows) for at, rows in zip(cuts, own)]
    pairs = [[((2, at), lower), ((0, at), upper)] for at, (lower, upper) in zip(cuts, back)]
    early += [pair for group in pairs[:-1] for pair in group]
    partial = partial_sum(selected, [rows for _, rows in early], tuple(at for at, _ in early))
    late = pairs[-1]
    out = finish(partial, rows_in, w_out, selected, [rows for _, rows in late], tuple(at for at, _ in late))
    return out.reshape(azim_cells, range_cells, width)


def solution(mesh):
    return jax.shard_map(
        shards,
        mesh=mesh,
        in_specs=(
            P("sector", "band", None),
            P(),
            P(),
            P(),
            P(),
            P(),
            P(("sector", "band"), None),
            P("sector", "band", None),
            P("sector", "band", None),
        ),
        out_specs=P("sector", "band", None),
        check_vma=False,
    )
```

```python
import functools

import jax
import jax.numpy as jnp
from jax import lax
from jax.experimental import pallas as pl
from jax.experimental.pallas import tpu as pltpu
from jax.sharding import PartitionSpec as P


HEADS = 8
BLK_DEV = 8
CAP = 128
LOG2_E = 1.4426950408889634
VMEM_BYTES = 24 << 20
UNROLL = 2


def params():
    return pltpu.CompilerParams(vmem_limit_bytes=VMEM_BYTES)


def shifted(block, axis, distance):
    count = lax.axis_size(axis)
    return lax.ppermute(block, axis, [(i, (i + distance) % count) for i in range(count)])


def swapped(block, axis, bit):
    count = lax.axis_size(axis)
    return lax.ppermute(block, axis, [(i, i ^ bit) for i in range(count)])


def fill_slots(codes_ref, rows, out_ref, first):
    queries = rows.shape[0]
    codes = codes_ref[...]
    slot = lax.broadcasted_iota(jnp.int32, (2 * CAP, queries), 0).astype(jnp.int16)
    one, zero = jnp.ones((), jnp.bfloat16), jnp.zeros((), jnp.bfloat16)
    for step in range(0, out_ref.shape[0], 2):
        near = (codes - (first + step) * CAP).astype(jnp.int16)
        hit = slot == near[0:1, :]
        for entry in range(1, codes.shape[0]):
            hit = hit | (slot == near[entry:entry + 1, :])
        got = jnp.dot(jnp.where(hit, one, zero), rows, preferred_element_type=jnp.float32).astype(jnp.bfloat16)
        out_ref[step:step + 2] = got.reshape(2, CAP, got.shape[1])


def project_kernel(codes_ref, queries_hbm, gain_hbm, weight_hbm, rows_ref, *refs):
    lower_ref, upper_ref, queries_ref, gain_ref, weight_ref, sems = refs
    copies = [
        pltpu.make_async_copy(source, target, sems.at[i])
        for i, (source, target) in enumerate(((queries_hbm, queries_ref), (gain_hbm, gain_ref), (weight_hbm, weight_ref)))
    ]
    for copy in copies:
        copy.start()
    for copy in copies:
        copy.wait()
    values = queries_ref[...].astype(jnp.float32)
    average = jnp.mean(values, axis=-1, keepdims=True)
    centred = values - average
    spread = jnp.mean(centred * centred, axis=-1, keepdims=True)
    normed = (centred * lax.rsqrt(spread + 1e-05) * gain_ref[...]).astype(jnp.bfloat16)
    rows = jnp.dot(normed, weight_ref[...], preferred_element_type=jnp.float32).astype(jnp.bfloat16)
    rows_ref[...] = rows
    fill_slots(codes_ref, rows, lower_ref, 2 * BLK_DEV)
    fill_slots(codes_ref, rows, upper_ref, 0)


def slot_shape(blocks, width):
    return jax.ShapeDtypeStruct((blocks, CAP, width), jnp.bfloat16)


def project(codes, queries, gain, weight, blocks):
    count, width = queries.shape
    hbm = pl.BlockSpec(memory_space=pltpu.HBM)
    return pl.pallas_call(
        project_kernel,
        in_specs=[pl.BlockSpec(memory_space=pltpu.VMEM), hbm, hbm, hbm],
        scratch_shapes=[
            pltpu.VMEM(queries.shape, queries.dtype),
            pltpu.VMEM(gain.shape, gain.dtype),
            pltpu.VMEM(weight.shape, weight.dtype),
            pltpu.SemaphoreType.DMA((3,)),
        ],
        out_shape=(jax.ShapeDtypeStruct((count, width), jnp.bfloat16),) + (slot_shape(blocks, width),) * 2,
        compiler_params=params(),
        cost_estimate=pl.CostEstimate(flops=4 << 30, bytes_accessed=2 << 20, transcendentals=0),
        name="project",
    )(codes, queries, gain, weight)


def scatter_kernel(codes_ref, rows_ref, own_ref, *refs, blocks):
    rows = rows_ref[...]
    for ref, first in zip(refs, (2 * BLK_DEV + blocks, blocks)):
        fill_slots(codes_ref, rows, ref, first)
    fill_slots(codes_ref, rows, own_ref, BLK_DEV)


def scatter(codes, rows, blocks):
    width = rows.shape[1]
    rest = BLK_DEV - blocks
    return pl.pallas_call(
        functools.partial(scatter_kernel, blocks=blocks),
        out_shape=(slot_shape(BLK_DEV, width),) + ((slot_shape(rest, width),) * 2 if rest else ()),
        compiler_params=params(),
        cost_estimate=pl.CostEstimate(flops=1 << 30, bytes_accessed=2 << 20, transcendentals=0),
        name="scatter",
    )(codes, rows)


def kv_kernel(key_ref, value_ref, *refs):
    out_ref = refs[-1]
    keys, width = out_ref.shape[1], key_ref.shape[1]
    done = 0
    for ref in refs[:-1]:
        for at in range(0, ref.shape[0], keys):
            rows = ref[at:at + keys]
            for side, weight_ref in enumerate((key_ref, value_ref)):
                got = jnp.dot(rows, weight_ref[...], preferred_element_type=jnp.float32)
                out_ref[done, :, side * width:(side + 1) * width] = got.astype(jnp.bfloat16)
            done += 1


def keys_and_values(features, w_key, w_value, keys):
    width = w_key.shape[1]
    count = sum(part.shape[0] for part in features)
    return pl.pallas_call(
        kv_kernel,
        out_shape=jax.ShapeDtypeStruct((count // keys, keys, 2 * width), jnp.bfloat16),
        compiler_params=params(),
        cost_estimate=pl.CostEstimate(flops=4 * count * width * width, bytes_accessed=6 * count * width, transcendentals=0),
        name="keys_and_values",
    )(w_key, w_value, *features)


def attend_kernel(rows_ref, kv_ref, out_ref, scores_ref, *, stack, start):
    blocks, (_, count, width) = kv_ref.shape[0], rows_ref.shape
    head_size = width // HEADS
    factor = head_size ** (-0.5) * LOG2_E
    head_of = lax.broadcasted_iota(jnp.int32, (1, width), 1) // head_size
    firsts = list(range(0, HEADS, stack))
    half = width // 2

    def scores_of(b, first):
        side = slice(half * (first >= HEADS // 2), half * (first >= HEADS // 2) + half)
        rows = rows_ref[start + b, :, side]
        kept = [jnp.where(head_of[:, side] == first + i, rows, jnp.zeros_like(rows)) for i in range(stack)]
        return lax.dot_general(
            jnp.concatenate(kept, axis=0), kv_ref[b, :, side],
            (((1,), (1,)), ((), ())), preferred_element_type=jnp.float32)

    scores_ref[...] = scores_of(0, 0)

    @pl.loop(0, blocks // UNROLL)
    def _(step):
        scores = scores_ref[...]
        for unit in range(UNROLL):
            b = step * UNROLL + unit
            merged = None
            for at, first in enumerate(firsts):
                if at + 1 < len(firsts):
                    following = scores_of(b, firsts[at + 1])
                else:
                    following = scores_of(jnp.minimum(b + 1, blocks - 1), 0)
                peak = jnp.max(scores, axis=1, keepdims=True)
                expo = jnp.exp2((scores - peak) * factor)
                weights = (expo * (1.0 / jnp.sum(expo, axis=1, keepdims=True))).astype(jnp.bfloat16)
                got = jnp.dot(weights, kv_ref[b, :, width:], preferred_element_type=jnp.float32)
                for i in range(stack):
                    part = got[i * count:(i + 1) * count]
                    merged = part if first + i == 0 else jnp.where(head_of == first + i, part, merged)
                scores = following
            out_ref[b] = merged.astype(jnp.bfloat16)
        scores_ref[...] = scores


def attend(rows, kv, start=0):
    _, count, width = rows.shape
    blocks, keys = kv.shape[:2]
    stack = 2
    pairs = blocks * count * keys
    return pl.pallas_call(
        functools.partial(attend_kernel, stack=stack, start=start),
        out_shape=jax.ShapeDtypeStruct((blocks, count, width), jnp.bfloat16),
        scratch_shapes=[pltpu.VMEM((stack * count, keys), jnp.float32)],
        compiler_params=params(),
        cost_estimate=pl.CostEstimate(
            flops=4 * pairs * width * HEADS, bytes_accessed=blocks * keys * width * 4,
            transcendentals=pairs * HEADS),
        name="attend",
    )(rows, kv)


def pick_kernel(codes_ref, *out_refs, groups):
    entries, count = codes_ref.shape
    spare = jnp.zeros((8 - entries, count), jnp.int32)
    at = jnp.concatenate([codes_ref[...], spare], axis=0).T
    lane = lax.broadcasted_iota(jnp.int32, (count, CAP), 1).astype(jnp.int16)
    near = [jnp.broadcast_to(at[:, entry:entry + 1], (count, CAP)).astype(jnp.int16) for entry in range(entries)]
    one, zero = jnp.ones((), jnp.bfloat16), jnp.zeros((), jnp.bfloat16)
    for group, out_ref in zip(groups, out_refs):
        for step in range(out_ref.shape[1] // CAP):
            slot = lane + jnp.int16(group * BLK_DEV * CAP + step * CAP)
            hit = slot == near[0]
            for entry in range(1, entries):
                hit = hit | (slot == near[entry])
            out_ref[:, step * CAP:(step + 1) * CAP] = jnp.where(hit, one, zero)


def picks(codes, groups):
    shape = jax.ShapeDtypeStruct((codes.shape[1], BLK_DEV * CAP), jnp.bfloat16)
    return pl.pallas_call(
        functools.partial(pick_kernel, groups=groups),
        out_shape=(shape,) * len(groups),
        compiler_params=params(),
        cost_estimate=pl.CostEstimate(flops=1 << 30, bytes_accessed=2 << 20, transcendentals=0),
        name="picks",
    )(codes)


def gathered(pick_refs, result_refs, places, rows):
    total = None
    for ref, (group, first) in zip(result_refs, places):
        slots = ref.shape[0] * ref.shape[1]
        got = jnp.dot(
            pick_refs[group][rows, first:first + slots], ref[...].reshape(slots, ref.shape[2]),
            preferred_element_type=jnp.float32)
        total = got if total is None else total + got
    return total


def partial_kernel(*refs, places):
    pick_refs, result_refs, out_ref = refs[:3], refs[3:-1], refs[-1]
    tile = 256
    for step in range(out_ref.shape[0] // tile):
        rows = slice(step * tile, (step + 1) * tile)
        out_ref[rows] = gathered(pick_refs, result_refs, places, rows)


def partial_sum(selected, results, places):
    return pl.pallas_call(
        functools.partial(partial_kernel, places=places),
        out_shape=jax.ShapeDtypeStruct((selected[0].shape[0], results[0].shape[2]), jnp.float32),
        compiler_params=params(),
        cost_estimate=pl.CostEstimate(flops=1 << 30, bytes_accessed=2 << 20, transcendentals=0),
        name="partial_sum",
    )(*selected, *results)


def final_kernel(partial_ref, queries_ref, weight_ref, *refs, places):
    pick_refs, result_refs, out_ref = refs[:3], refs[3:-1], refs[-1]
    tile = 256
    for step in range(out_ref.shape[0] // tile):
        rows = slice(step * tile, (step + 1) * tile)
        total = partial_ref[rows] + gathered(pick_refs, result_refs, places, rows)
        final = jnp.dot(total.astype(jnp.bfloat16), weight_ref[...], preferred_element_type=jnp.float32)
        out_ref[rows] = (final + queries_ref[rows].astype(jnp.float32)).astype(jnp.bfloat16)


def finish(partial, queries, weight, selected, results, places):
    return pl.pallas_call(
        functools.partial(final_kernel, places=places),
        out_shape=jax.ShapeDtypeStruct(queries.shape, jnp.bfloat16),
        compiler_params=params(),
        cost_estimate=pl.CostEstimate(flops=1 << 30, bytes_accessed=2 << 20, transcendentals=0),
        name="finish",
    )(partial, queries, weight, *selected, *results)


def shards(queries, norm_gain, w_query, w_key, w_value, w_out, features, visible, live):
    azim_cells, range_cells, width = queries.shape
    entries = visible.shape[2]
    count = azim_cells * range_cells
    bands = lax.axis_size("band")
    local_rows = features.shape[0]
    keys = bands * local_rows // BLK_DEV
    staged = bands == 4 and local_rows == 2 * keys

    shift = (lax.axis_index("band") * local_rows // keys) * CAP
    codes = jnp.where(live != 0, visible ^ shift, -1).transpose(2, 0, 1).reshape(entries, count)
    rows_in = queries.reshape(count, width)

    if staged:
        across = swapped(features, "band", 2)
        held = [[features, swapped(features, "band", 1)]]
    else:
        whole_sector = features
        bit = 1
        while bit < bands:
            whole_sector = jnp.concatenate([whole_sector, swapped(whole_sector, "band", bit)], axis=0)
            bit *= 2
        held = [[whole_sector]]
    selected = picks(codes, (0, 1, 2))
    codes, *selected = lax.optimization_barrier((codes, *selected))
    blocks = BLK_DEV // 2 if staged else BLK_DEV
    projected, *ready = project(codes, rows_in, norm_gain.reshape(1, width), w_query, blocks)

    def send(lower, upper):
        lower = shifted(lower, "sector", 1)
        return lower, shifted(upper, "sector", -1)

    visits = [send(*ready)]
    projected, *_ = lax.optimization_barrier((projected, *ready))
    slots_own, *ready = scatter(codes, projected, blocks)
    kvs = [keys_and_values(held[0], w_key, w_value, keys)]
    own = [attend(slots_own, kvs[0])]
    last = own[0]
    if staged:
        *ready, last = lax.optimization_barrier((*ready, last))
        visits.append(send(*ready))
    back = []
    for part, (lower, upper) in enumerate(visits):
        if part:
            kvs.append(keys_and_values([across, beyond], w_key, w_value, keys))
        lower, last = lax.optimization_barrier((lower, last))
        lower = attend(lower, kvs[part])
        upper, lower = lax.optimization_barrier((upper, lower))
        upper = attend(upper, kvs[part])
        if staged and not part:
            lower, upper, across = lax.optimization_barrier((lower, upper, across))
            beyond = swapped(across, "band", 1)
        lower = shifted(lower, "sector", -1)
        last = upper
        upper = shifted(upper, "sector", 1)
        back.append((lower, upper))
    if staged:
        turn, last = lax.optimization_barrier((slots_own, last))
        own.append(attend(turn, kvs[1], blocks))

    cuts = [i * blocks * CAP for i in range(len(kvs))]
    early = [((1, at), rows) for at, rows in zip(cuts, own)]
    returned = [((2, at), lower) for at, (lower, _) in zip(cuts, back)]
    returned += [((0, at), upper) for at, (_, upper) in zip(cuts, back)]
    early += returned[:-1]
    partial = partial_sum(selected, [rows for _, rows in early], tuple(at for at, _ in early))
    late = returned[-1:]
    out = finish(partial, rows_in, w_out, selected, [rows for _, rows in late], tuple(at for at, _ in late))
    return out.reshape(azim_cells, range_cells, width)


def solution(mesh):
    return jax.shard_map(
        shards,
        mesh=mesh,
        in_specs=(
            P("sector", "band", None),
            P(),
            P(),
            P(),
            P(),
            P(),
            P(("sector", "band"), None),
            P("sector", "band", None),
            P("sector", "band", None),
        ),
        out_specs=P("sector", "band", None),
        check_vma=False,
    )
```

```python
import functools

import jax
import jax.numpy as jnp
from jax import lax
from jax.experimental import pallas as pl
from jax.experimental.pallas import tpu as pltpu
from jax.sharding import PartitionSpec as P


HEADS = 8
BLK_DEV = 8
CAP = 128
LOG2_E = 1.4426950408889634
VMEM_BYTES = 24 << 20
UNROLL = 2


def params():
    return pltpu.CompilerParams(vmem_limit_bytes=VMEM_BYTES)


def exchanged(block, side):
    count = lax.axis_size("sector")
    return lax.ppermute(block, "sector", [(i, (((i + side) ^ 1) - side) % count) for i in range(count)])


def swapped(block, axis, bit):
    count = lax.axis_size(axis)
    return lax.ppermute(block, axis, [(i, i ^ bit) for i in range(count)])


def fill_slots(codes_ref, rows, out_ref, first):
    queries = rows.shape[0]
    codes = codes_ref[...]
    slot = lax.broadcasted_iota(jnp.int32, (2 * CAP, queries), 0).astype(jnp.int16)
    one, zero = jnp.ones((), jnp.bfloat16), jnp.zeros((), jnp.bfloat16)
    for step in range(0, out_ref.shape[0], 2):
        near = (codes - (first + step) * CAP).astype(jnp.int16)
        hit = slot == near[0:1, :]
        for entry in range(1, codes.shape[0]):
            hit = hit | (slot == near[entry:entry + 1, :])
        got = jnp.dot(jnp.where(hit, one, zero), rows, preferred_element_type=jnp.float32).astype(jnp.bfloat16)
        out_ref[step:step + 2] = got.reshape(2, CAP, got.shape[1])


def project_kernel(codes_ref, queries_hbm, gain_hbm, weight_hbm, rows_ref, *refs):
    lower_ref, upper_ref, queries_ref, gain_ref, weight_ref, sems = refs
    copies = [
        pltpu.make_async_copy(source, target, sems.at[i])
        for i, (source, target) in enumerate(((queries_hbm, queries_ref), (gain_hbm, gain_ref), (weight_hbm, weight_ref)))
    ]
    for copy in copies:
        copy.start()
    for copy in copies:
        copy.wait()
    values = queries_ref[...].astype(jnp.float32)
    average = jnp.mean(values, axis=-1, keepdims=True)
    centred = values - average
    spread = jnp.mean(centred * centred, axis=-1, keepdims=True)
    normed = (centred * lax.rsqrt(spread + 1e-05) * gain_ref[...]).astype(jnp.bfloat16)
    rows = jnp.dot(normed, weight_ref[...], preferred_element_type=jnp.float32).astype(jnp.bfloat16)
    rows_ref[...] = rows
    fill_slots(codes_ref, rows, lower_ref, 2 * BLK_DEV)
    fill_slots(codes_ref, rows, upper_ref, 0)


def slot_shape(blocks, width):
    return jax.ShapeDtypeStruct((blocks, CAP, width), jnp.bfloat16)


def project(codes, queries, gain, weight, blocks):
    count, width = queries.shape
    hbm = pl.BlockSpec(memory_space=pltpu.HBM)
    return pl.pallas_call(
        project_kernel,
        in_specs=[pl.BlockSpec(memory_space=pltpu.VMEM), hbm, hbm, hbm],
        scratch_shapes=[
            pltpu.VMEM(queries.shape, queries.dtype),
            pltpu.VMEM(gain.shape, gain.dtype),
            pltpu.VMEM(weight.shape, weight.dtype),
            pltpu.SemaphoreType.DMA((3,)),
        ],
        out_shape=(jax.ShapeDtypeStruct((count, width), jnp.bfloat16),) + (slot_shape(blocks, width),) * 2,
        compiler_params=params(),
        cost_estimate=pl.CostEstimate(flops=4 << 30, bytes_accessed=2 << 20, transcendentals=0),
        name="project",
    )(codes, queries, gain, weight)


def scatter_kernel(codes_ref, rows_ref, own_ref, *refs, blocks):
    rows = rows_ref[...]
    for ref, first in zip(refs, (2 * BLK_DEV + blocks, blocks)):
        fill_slots(codes_ref, rows, ref, first)
    fill_slots(codes_ref, rows, own_ref, BLK_DEV)


def scatter(codes, rows, blocks):
    width = rows.shape[1]
    rest = BLK_DEV - blocks
    return pl.pallas_call(
        functools.partial(scatter_kernel, blocks=blocks),
        out_shape=(slot_shape(BLK_DEV, width),) + ((slot_shape(rest, width),) * 2 if rest else ()),
        compiler_params=params(),
        cost_estimate=pl.CostEstimate(flops=1 << 30, bytes_accessed=2 << 20, transcendentals=0),
        name="scatter",
    )(codes, rows)


def kv_kernel(key_ref, value_ref, *refs):
    out_ref = refs[-1]
    keys, width = out_ref.shape[1], key_ref.shape[1]
    done = 0
    for ref in refs[:-1]:
        for at in range(0, ref.shape[0], keys):
            rows = ref[at:at + keys]
            for side, weight_ref in enumerate((key_ref, value_ref)):
                got = jnp.dot(rows, weight_ref[...], preferred_element_type=jnp.float32)
                out_ref[done, :, side * width:(side + 1) * width] = got.astype(jnp.bfloat16)
            done += 1


def keys_and_values(features, w_key, w_value, keys):
    width = w_key.shape[1]
    count = sum(part.shape[0] for part in features)
    return pl.pallas_call(
        kv_kernel,
        out_shape=jax.ShapeDtypeStruct((count // keys, keys, 2 * width), jnp.bfloat16),
        compiler_params=params(),
        cost_estimate=pl.CostEstimate(flops=4 * count * width * width, bytes_accessed=6 * count * width, transcendentals=0),
        name="keys_and_values",
    )(w_key, w_value, *features)


def attend_kernel(rows_ref, kv_ref, out_ref, scores_ref, *, stack, start):
    blocks, (_, count, width) = kv_ref.shape[0], rows_ref.shape
    head_size = width // HEADS
    factor = head_size ** (-0.5) * LOG2_E
    head_of = lax.broadcasted_iota(jnp.int32, (1, width), 1) // head_size
    firsts = list(range(0, HEADS, stack))
    half = width // 2

    def scores_of(b, first):
        side = slice(half * (first >= HEADS // 2), half * (first >= HEADS // 2) + half)
        rows = rows_ref[start + b, :, side]
        kept = [jnp.where(head_of[:, side] == first + i, rows, jnp.zeros_like(rows)) for i in range(stack)]
        return lax.dot_general(
            jnp.concatenate(kept, axis=0), kv_ref[b, :, side],
            (((1,), (1,)), ((), ())), preferred_element_type=jnp.float32)

    scores_ref[...] = scores_of(0, 0)

    @pl.loop(0, blocks // UNROLL)
    def _(step):
        scores = scores_ref[...]
        for unit in range(UNROLL):
            b = step * UNROLL + unit
            merged = None
            for at, first in enumerate(firsts):
                if at + 1 < len(firsts):
                    following = scores_of(b, firsts[at + 1])
                else:
                    following = scores_of(jnp.minimum(b + 1, blocks - 1), 0)
                peak = jnp.max(scores, axis=1, keepdims=True)
                expo = jnp.exp2((scores - peak) * factor)
                weights = (expo * (1.0 / jnp.sum(expo, axis=1, keepdims=True))).astype(jnp.bfloat16)
                got = jnp.dot(weights, kv_ref[b, :, width:], preferred_element_type=jnp.float32)
                for i in range(stack):
                    part = got[i * count:(i + 1) * count]
                    merged = part if first + i == 0 else jnp.where(head_of == first + i, part, merged)
                scores = following
            out_ref[b] = merged.astype(jnp.bfloat16)
        scores_ref[...] = scores


def attend(rows, kv, start=0):
    _, count, width = rows.shape
    blocks, keys = kv.shape[:2]
    stack = 2
    pairs = blocks * count * keys
    return pl.pallas_call(
        functools.partial(attend_kernel, stack=stack, start=start),
        out_shape=jax.ShapeDtypeStruct((blocks, count, width), jnp.bfloat16),
        scratch_shapes=[pltpu.VMEM((stack * count, keys), jnp.float32)],
        compiler_params=params(),
        cost_estimate=pl.CostEstimate(
            flops=4 * pairs * width * HEADS, bytes_accessed=blocks * keys * width * 4,
            transcendentals=pairs * HEADS),
        name="attend",
    )(rows, kv)


def pick_kernel(codes_ref, *out_refs, groups):
    entries, count = codes_ref.shape
    spare = jnp.zeros((8 - entries, count), jnp.int32)
    at = jnp.concatenate([codes_ref[...], spare], axis=0).T
    lane = lax.broadcasted_iota(jnp.int32, (count, CAP), 1).astype(jnp.int16)
    near = [jnp.broadcast_to(at[:, entry:entry + 1], (count, CAP)).astype(jnp.int16) for entry in range(entries)]
    one, zero = jnp.ones((), jnp.bfloat16), jnp.zeros((), jnp.bfloat16)
    for group, out_ref in zip(groups, out_refs):
        for step in range(out_ref.shape[1] // CAP):
            slot = lane + jnp.int16(group * BLK_DEV * CAP + step * CAP)
            hit = slot == near[0]
            for entry in range(1, entries):
                hit = hit | (slot == near[entry])
            out_ref[:, step * CAP:(step + 1) * CAP] = jnp.where(hit, one, zero)


def picks(codes, groups):
    shape = jax.ShapeDtypeStruct((codes.shape[1], BLK_DEV * CAP), jnp.bfloat16)
    return pl.pallas_call(
        functools.partial(pick_kernel, groups=groups),
        out_shape=(shape,) * len(groups),
        compiler_params=params(),
        cost_estimate=pl.CostEstimate(flops=1 << 30, bytes_accessed=2 << 20, transcendentals=0),
        name="picks",
    )(codes)


def gathered(pick_refs, result_refs, places, rows):
    total = None
    for ref, (group, first) in zip(result_refs, places):
        slots = ref.shape[0] * ref.shape[1]
        got = jnp.dot(
            pick_refs[group][rows, first:first + slots], ref[...].reshape(slots, ref.shape[2]),
            preferred_element_type=jnp.float32)
        total = got if total is None else total + got
    return total


def partial_kernel(*refs, places):
    pick_refs, result_refs, out_ref = refs[:3], refs[3:-1], refs[-1]
    tile = 256
    for step in range(out_ref.shape[0] // tile):
        rows = slice(step * tile, (step + 1) * tile)
        out_ref[rows] = gathered(pick_refs, result_refs, places, rows)


def partial_sum(selected, results, places):
    return pl.pallas_call(
        functools.partial(partial_kernel, places=places),
        out_shape=jax.ShapeDtypeStruct((selected[0].shape[0], results[0].shape[2]), jnp.float32),
        compiler_params=params(),
        cost_estimate=pl.CostEstimate(flops=1 << 30, bytes_accessed=2 << 20, transcendentals=0),
        name="partial_sum",
    )(*selected, *results)


def final_kernel(partial_ref, queries_ref, weight_ref, *refs, places):
    pick_refs, result_refs, out_ref = refs[:3], refs[3:-1], refs[-1]
    tile = 256
    for step in range(out_ref.shape[0] // tile):
        rows = slice(step * tile, (step + 1) * tile)
        total = partial_ref[rows] + gathered(pick_refs, result_refs, places, rows)
        final = jnp.dot(total.astype(jnp.bfloat16), weight_ref[...], preferred_element_type=jnp.float32)
        out_ref[rows] = (final + queries_ref[rows].astype(jnp.float32)).astype(jnp.bfloat16)


def finish(partial, queries, weight, selected, results, places):
    return pl.pallas_call(
        functools.partial(final_kernel, places=places),
        out_shape=jax.ShapeDtypeStruct(queries.shape, jnp.bfloat16),
        compiler_params=params(),
        cost_estimate=pl.CostEstimate(flops=1 << 30, bytes_accessed=2 << 20, transcendentals=0),
        name="finish",
    )(partial, queries, weight, *selected, *results)


def shards(queries, norm_gain, w_query, w_key, w_value, w_out, features, visible, live):
    azim_cells, range_cells, width = queries.shape
    entries = visible.shape[2]
    count = azim_cells * range_cells
    bands = lax.axis_size("band")
    local_rows = features.shape[0]
    keys = bands * local_rows // BLK_DEV
    staged = bands == 4 and local_rows == 2 * keys

    shift = (lax.axis_index("band") * local_rows // keys) * CAP
    span = BLK_DEV * CAP
    turned = visible + (2 - 2 * lax.div(visible, span)) * span
    named = jnp.where(lax.axis_index("sector") % 2 == 1, turned, visible)
    codes = jnp.where(live != 0, named ^ shift, -1).transpose(2, 0, 1).reshape(entries, count)
    rows_in = queries.reshape(count, width)

    if staged:
        across = swapped(features, "band", 2)
        held = [[features, swapped(features, "band", 1)]]
    else:
        whole_sector = features
        bit = 1
        while bit < bands:
            whole_sector = jnp.concatenate([whole_sector, swapped(whole_sector, "band", bit)], axis=0)
            bit *= 2
        held = [[whole_sector]]
    selected = picks(codes, (0, 1, 2))
    codes, *selected = lax.optimization_barrier((codes, *selected))
    blocks = BLK_DEV // 2 if staged else BLK_DEV
    projected, *ready = project(codes, rows_in, norm_gain.reshape(1, width), w_query, blocks)

    def send(lower, upper):
        lower = exchanged(lower, 0)
        return lower, exchanged(upper, 1)

    visits = [send(*ready)]
    projected, *_ = lax.optimization_barrier((projected, *ready))
    slots_own, *ready = scatter(codes, projected, blocks)
    kvs = [keys_and_values(held[0], w_key, w_value, keys)]
    own = [attend(slots_own, kvs[0])]
    last = own[0]
    if staged:
        *ready, last = lax.optimization_barrier((*ready, last))
        visits.append(send(*ready))
    back = []
    for part, (lower, upper) in enumerate(visits):
        if part:
            kvs.append(keys_and_values([across, beyond], w_key, w_value, keys))
        arrived = {"lower": lower, "upper": upper}
        turns = ("upper", "lower") if part else ("lower", "upper")
        for name in turns:
            rows, last = lax.optimization_barrier((arrived[name], last))
            last = arrived[name] = attend(rows, kvs[part])
            if staged and part == 0 and name == turns[0]:
                across, last = lax.optimization_barrier((across, last))
                beyond = swapped(across, "band", 1)
        if staged and not part:
            arrived = dict(zip(arrived, lax.optimization_barrier(tuple(arrived.values()))))
        for side, name in enumerate(("lower", "upper")):
            arrived[name] = exchanged(arrived[name], side)
        back.append((arrived["lower"], arrived["upper"]))
    if staged:
        turn, last = lax.optimization_barrier((slots_own, last))
        own.append(attend(turn, kvs[1], blocks))

    cuts = [i * blocks * CAP for i in range(len(kvs))]
    early = [((1, at), rows) for at, rows in zip(cuts, own)]
    returned = [((0, at), upper) for at, (_, upper) in zip(cuts, back)]
    returned += [((2, at), lower) for at, (lower, _) in zip(cuts, back)]
    early += returned[:-1]
    partial = partial_sum(selected, [rows for _, rows in early], tuple(at for at, _ in early))
    late = returned[-1:]
    out = finish(partial, rows_in, w_out, selected, [rows for _, rows in late], tuple(at for at, _ in late))
    return out.reshape(azim_cells, range_cells, width)


def solution(mesh):
    return jax.shard_map(
        shards,
        mesh=mesh,
        in_specs=(
            P("sector", "band", None),
            P(),
            P(),
            P(),
            P(),
            P(),
            P(("sector", "band"), None),
            P("sector", "band", None),
            P("sector", "band", None),
        ),
        out_specs=P("sector", "band", None),
        check_vma=False,
    )
```

```python
import functools

import jax
import jax.numpy as jnp
from jax import lax
from jax.experimental import pallas as pl
from jax.experimental.pallas import tpu as pltpu
from jax.sharding import PartitionSpec as P


HEADS = 8
BLK_DEV = 8
CAP = 128
LOG2_E = 1.4426950408889634
VMEM_BYTES = 24 << 20
UNROLL = 2


def params():
    return pltpu.CompilerParams(vmem_limit_bytes=VMEM_BYTES)


def exchanged(block, side):
    count = lax.axis_size("sector")
    return lax.ppermute(block, "sector", [(i, (((i + side) ^ 1) - side) % count) for i in range(count)])


def swapped(block, axis, bit):
    count = lax.axis_size(axis)
    return lax.ppermute(block, axis, [(i, i ^ bit) for i in range(count)])


def fill_slots(codes_ref, rows, out_ref, first):
    queries = rows.shape[0]
    codes = codes_ref[...]
    slot = lax.broadcasted_iota(jnp.int32, (2 * CAP, queries), 0).astype(jnp.int16)
    one, zero = jnp.ones((), jnp.bfloat16), jnp.zeros((), jnp.bfloat16)
    for step in range(0, out_ref.shape[0], 2):
        near = (codes - (first + step) * CAP).astype(jnp.int16)
        hit = slot == near[0:1, :]
        for entry in range(1, codes.shape[0]):
            hit = hit | (slot == near[entry:entry + 1, :])
        got = jnp.dot(jnp.where(hit, one, zero), rows, preferred_element_type=jnp.float32).astype(jnp.bfloat16)
        out_ref[step:step + 2] = got.reshape(2, CAP, got.shape[1])


def project_kernel(codes_ref, queries_hbm, gain_hbm, weight_hbm, rows_ref, *refs):
    lower_ref, upper_ref, queries_ref, gain_ref, weight_ref, sems = refs
    copies = [
        pltpu.make_async_copy(source, target, sems.at[i])
        for i, (source, target) in enumerate(((queries_hbm, queries_ref), (gain_hbm, gain_ref), (weight_hbm, weight_ref)))
    ]
    for copy in copies:
        copy.start()
    for copy in copies:
        copy.wait()
    values = queries_ref[...].astype(jnp.float32)
    average = jnp.mean(values, axis=-1, keepdims=True)
    centred = values - average
    spread = jnp.mean(centred * centred, axis=-1, keepdims=True)
    normed = (centred * lax.rsqrt(spread + 1e-05) * gain_ref[...]).astype(jnp.bfloat16)
    rows = jnp.dot(normed, weight_ref[...], preferred_element_type=jnp.float32).astype(jnp.bfloat16)
    rows_ref[...] = rows
    fill_slots(codes_ref, rows, lower_ref, 2 * BLK_DEV)
    fill_slots(codes_ref, rows, upper_ref, 0)


def slot_shape(blocks, width):
    return jax.ShapeDtypeStruct((blocks, CAP, width), jnp.bfloat16)


def project(codes, queries, gain, weight, blocks):
    count, width = queries.shape
    hbm = pl.BlockSpec(memory_space=pltpu.HBM)
    return pl.pallas_call(
        project_kernel,
        in_specs=[pl.BlockSpec(memory_space=pltpu.VMEM), hbm, hbm, hbm],
        scratch_shapes=[
            pltpu.VMEM(queries.shape, queries.dtype),
            pltpu.VMEM(gain.shape, gain.dtype),
            pltpu.VMEM(weight.shape, weight.dtype),
            pltpu.SemaphoreType.DMA((3,)),
        ],
        out_shape=(
            jax.ShapeDtypeStruct((count, width), jnp.bfloat16),
            slot_shape(blocks, width),
            slot_shape(BLK_DEV, width),
        ),
        compiler_params=params(),
        cost_estimate=pl.CostEstimate(flops=4 << 30, bytes_accessed=2 << 20, transcendentals=0),
        name="project",
    )(codes, queries, gain, weight)


def scatter_kernel(codes_ref, rows_ref, own_ref, *refs, blocks):
    rows = rows_ref[...]
    for ref in refs:
        fill_slots(codes_ref, rows, ref, 2 * BLK_DEV + blocks)
    fill_slots(codes_ref, rows, own_ref, BLK_DEV)


def scatter(codes, rows, blocks):
    width = rows.shape[1]
    rest = BLK_DEV - blocks
    return pl.pallas_call(
        functools.partial(scatter_kernel, blocks=blocks),
        out_shape=(slot_shape(BLK_DEV, width),) + ((slot_shape(rest, width),) if rest else ()),
        compiler_params=params(),
        cost_estimate=pl.CostEstimate(flops=1 << 30, bytes_accessed=2 << 20, transcendentals=0),
        name="scatter",
    )(codes, rows)


def kv_kernel(key_ref, value_ref, *refs):
    out_ref = refs[-1]
    keys, width = out_ref.shape[1], key_ref.shape[1]
    done = 0
    for ref in refs[:-1]:
        for at in range(0, ref.shape[0], keys):
            rows = ref[at:at + keys]
            for side, weight_ref in enumerate((key_ref, value_ref)):
                got = jnp.dot(rows, weight_ref[...], preferred_element_type=jnp.float32)
                out_ref[done, :, side * width:(side + 1) * width] = got.astype(jnp.bfloat16)
            done += 1


def keys_and_values(features, w_key, w_value, keys):
    width = w_key.shape[1]
    count = sum(part.shape[0] for part in features)
    return pl.pallas_call(
        kv_kernel,
        out_shape=jax.ShapeDtypeStruct((count // keys, keys, 2 * width), jnp.bfloat16),
        compiler_params=params(),
        cost_estimate=pl.CostEstimate(flops=4 * count * width * width, bytes_accessed=6 * count * width, transcendentals=0),
        name="keys_and_values",
    )(w_key, w_value, *features)


def attend_kernel(rows_ref, kv_ref, out_ref, scores_ref, *, stack, start):
    blocks, (_, count, width) = kv_ref.shape[0], rows_ref.shape
    head_size = width // HEADS
    factor = head_size ** (-0.5) * LOG2_E
    head_of = lax.broadcasted_iota(jnp.int32, (1, width), 1) // head_size
    firsts = list(range(0, HEADS, stack))
    half = width // 2

    def scores_of(b, first):
        side = slice(half * (first >= HEADS // 2), half * (first >= HEADS // 2) + half)
        rows = rows_ref[start + b, :, side]
        kept = [jnp.where(head_of[:, side] == first + i, rows, jnp.zeros_like(rows)) for i in range(stack)]
        return lax.dot_general(
            jnp.concatenate(kept, axis=0), kv_ref[b, :, side],
            (((1,), (1,)), ((), ())), preferred_element_type=jnp.float32)

    scores_ref[...] = scores_of(0, 0)

    @pl.loop(0, blocks // UNROLL)
    def _(step):
        scores = scores_ref[...]
        for unit in range(UNROLL):
            b = step * UNROLL + unit
            merged = None
            for at, first in enumerate(firsts):
                if at + 1 < len(firsts):
                    following = scores_of(b, firsts[at + 1])
                else:
                    following = scores_of(jnp.minimum(b + 1, blocks - 1), 0)
                peak = jnp.max(scores, axis=1, keepdims=True)
                expo = jnp.exp2((scores - peak) * factor)
                weights = (expo * (1.0 / jnp.sum(expo, axis=1, keepdims=True))).astype(jnp.bfloat16)
                got = jnp.dot(weights, kv_ref[b, :, width:], preferred_element_type=jnp.float32)
                for i in range(stack):
                    part = got[i * count:(i + 1) * count]
                    merged = part if first + i == 0 else jnp.where(head_of == first + i, part, merged)
                scores = following
            out_ref[b] = merged.astype(jnp.bfloat16)
        scores_ref[...] = scores


def attend(rows, kv, start=0):
    _, count, width = rows.shape
    blocks, keys = kv.shape[:2]
    stack = 2
    pairs = blocks * count * keys
    return pl.pallas_call(
        functools.partial(attend_kernel, stack=stack, start=start),
        out_shape=jax.ShapeDtypeStruct((blocks, count, width), jnp.bfloat16),
        scratch_shapes=[pltpu.VMEM((stack * count, keys), jnp.float32)],
        compiler_params=params(),
        cost_estimate=pl.CostEstimate(
            flops=4 * pairs * width * HEADS, bytes_accessed=blocks * keys * width * 4,
            transcendentals=pairs * HEADS),
        name="attend",
    )(rows, kv)


def pick_kernel(codes_ref, *out_refs, groups):
    entries, count = codes_ref.shape
    spare = jnp.zeros((8 - entries, count), jnp.int32)
    at = jnp.concatenate([codes_ref[...], spare], axis=0).T
    lane = lax.broadcasted_iota(jnp.int32, (count, CAP), 1).astype(jnp.int16)
    near = [jnp.broadcast_to(at[:, entry:entry + 1], (count, CAP)).astype(jnp.int16) for entry in range(entries)]
    one, zero = jnp.ones((), jnp.bfloat16), jnp.zeros((), jnp.bfloat16)
    for group, out_ref in zip(groups, out_refs):
        for step in range(out_ref.shape[1] // CAP):
            slot = lane + jnp.int16(group * BLK_DEV * CAP + step * CAP)
            hit = slot == near[0]
            for entry in range(1, entries):
                hit = hit | (slot == near[entry])
            out_ref[:, step * CAP:(step + 1) * CAP] = jnp.where(hit, one, zero)


def picks(codes, groups):
    shape = jax.ShapeDtypeStruct((codes.shape[1], BLK_DEV * CAP), jnp.bfloat16)
    return pl.pallas_call(
        functools.partial(pick_kernel, groups=groups),
        out_shape=(shape,) * len(groups),
        compiler_params=params(),
        cost_estimate=pl.CostEstimate(flops=1 << 30, bytes_accessed=2 << 20, transcendentals=0),
        name="picks",
    )(codes)


def gathered(pick_refs, result_refs, places, rows):
    total = None
    for ref, (group, first) in zip(result_refs, places):
        slots = ref.shape[0] * ref.shape[1]
        got = jnp.dot(
            pick_refs[group][rows, first:first + slots], ref[...].reshape(slots, ref.shape[2]),
            preferred_element_type=jnp.float32)
        total = got if total is None else total + got
    return total


def partial_kernel(*refs, places):
    pick_refs, result_refs, out_ref = refs[:3], refs[3:-1], refs[-1]
    tile = 256
    for step in range(out_ref.shape[0] // tile):
        rows = slice(step * tile, (step + 1) * tile)
        out_ref[rows] = gathered(pick_refs, result_refs, places, rows)


def partial_sum(selected, results, places):
    return pl.pallas_call(
        functools.partial(partial_kernel, places=places),
        out_shape=jax.ShapeDtypeStruct((selected[0].shape[0], results[0].shape[2]), jnp.float32),
        compiler_params=params(),
        cost_estimate=pl.CostEstimate(flops=1 << 30, bytes_accessed=2 << 20, transcendentals=0),
        name="partial_sum",
    )(*selected, *results)


def final_kernel(partial_ref, queries_ref, weight_ref, *refs, places):
    pick_refs, result_refs, out_ref = refs[:3], refs[3:-1], refs[-1]
    tile = 256
    for step in range(out_ref.shape[0] // tile):
        rows = slice(step * tile, (step + 1) * tile)
        total = partial_ref[rows] + gathered(pick_refs, result_refs, places, rows)
        final = jnp.dot(total.astype(jnp.bfloat16), weight_ref[...], preferred_element_type=jnp.float32)
        out_ref[rows] = (final + queries_ref[rows].astype(jnp.float32)).astype(jnp.bfloat16)


def finish(partial, queries, weight, selected, results, places):
    return pl.pallas_call(
        functools.partial(final_kernel, places=places),
        out_shape=jax.ShapeDtypeStruct(queries.shape, jnp.bfloat16),
        compiler_params=params(),
        cost_estimate=pl.CostEstimate(flops=1 << 30, bytes_accessed=2 << 20, transcendentals=0),
        name="finish",
    )(partial, queries, weight, *selected, *results)


def shards(queries, norm_gain, w_query, w_key, w_value, w_out, features, visible, live):
    azim_cells, range_cells, width = queries.shape
    entries = visible.shape[2]
    count = azim_cells * range_cells
    bands = lax.axis_size("band")
    local_rows = features.shape[0]
    keys = bands * local_rows // BLK_DEV
    staged = bands == 4 and local_rows == 2 * keys

    shift = (lax.axis_index("band") * local_rows // keys) * CAP
    span = BLK_DEV * CAP
    turned = visible + (2 - 2 * lax.div(visible, span)) * span
    named = jnp.where(lax.axis_index("sector") % 2 == 1, turned, visible)
    codes = jnp.where(live != 0, named ^ shift, -1).transpose(2, 0, 1).reshape(entries, count)
    rows_in = queries.reshape(count, width)

    if staged:
        across = swapped(features, "band", 2)
        held = [[features, swapped(features, "band", 1)]]
    else:
        whole_sector = features
        bit = 1
        while bit < bands:
            whole_sector = jnp.concatenate([whole_sector, swapped(whole_sector, "band", bit)], axis=0)
            bit *= 2
        held = [[whole_sector]]
    selected = picks(codes, (0, 1, 2))
    codes, *selected = lax.optimization_barrier((codes, *selected))
    blocks = BLK_DEV // 2 if staged else BLK_DEV
    projected, *ready = project(codes, rows_in, norm_gain.reshape(1, width), w_query, blocks)

    lowers = [exchanged(ready[0], 0)]
    upper = exchanged(ready[1], 1)
    projected, *_ = lax.optimization_barrier((projected, *ready))
    slots_own, *ready = scatter(codes, projected, blocks)
    kvs = [keys_and_values(held[0], w_key, w_value, keys)]
    own = [attend(slots_own, kvs[0])]
    last = own[0]
    if staged:
        *ready, last = lax.optimization_barrier((*ready, last))
        lowers.append(exchanged(ready[0], 0))
    back = []
    for part, lower in enumerate(lowers):
        if part:
            kvs.append(keys_and_values([across, beyond], w_key, w_value, keys))
        arrived = {"lower": lower, "upper": upper}
        starts = {"lower": 0, "upper": part * blocks}
        turns = ("upper", "lower") if part else ("lower", "upper")
        for name in turns:
            rows, last = lax.optimization_barrier((arrived[name], last))
            last = arrived[name] = attend(rows, kvs[part], starts[name])
        if staged and not part:
            *both, across = lax.optimization_barrier((*arrived.values(), across))
            arrived = dict(zip(arrived, both))
            beyond = swapped(across, "band", 1)
        for side, name in enumerate(("lower", "upper")):
            arrived[name] = exchanged(arrived[name], side)
        back.append((arrived["lower"], arrived["upper"]))
    if staged:
        turn, last = lax.optimization_barrier((slots_own, last))
        own.append(attend(turn, kvs[1], blocks))

    cuts = [i * blocks * CAP for i in range(len(kvs))]
    early = [((1, at), rows) for at, rows in zip(cuts, own)]
    returned = [((0, at), upper) for at, (_, upper) in zip(cuts, back)]
    returned += [((2, at), lower) for at, (lower, _) in zip(cuts, back)]
    early += returned[:-1]
    partial = partial_sum(selected, [rows for _, rows in early], tuple(at for at, _ in early))
    late = returned[-1:]
    out = finish(partial, rows_in, w_out, selected, [rows for _, rows in late], tuple(at for at, _ in late))
    return out.reshape(azim_cells, range_cells, width)


def solution(mesh):
    return jax.shard_map(
        shards,
        mesh=mesh,
        in_specs=(
            P("sector", "band", None),
            P(),
            P(),
            P(),
            P(),
            P(),
            P(("sector", "band"), None),
            P("sector", "band", None),
            P("sector", "band", None),
        ),
        out_specs=P("sector", "band", None),
        check_vma=False,
    )
```

```python
import functools

import jax
import jax.numpy as jnp
from jax import lax
from jax.experimental import pallas as pl
from jax.experimental.pallas import tpu as pltpu
from jax.sharding import PartitionSpec as P


HEADS = 8
BLK_DEV = 8
CAP = 128
LOG2_E = 1.4426950408889634
VMEM_BYTES = 24 << 20
UNROLL = 2


def params():
    return pltpu.CompilerParams(vmem_limit_bytes=VMEM_BYTES)


def exchanged(block, side):
    count = lax.axis_size("sector")
    return lax.ppermute(block, "sector", [(i, (((i + side) ^ 1) - side) % count) for i in range(count)])


def swapped(block, axis, bit):
    count = lax.axis_size(axis)
    return lax.ppermute(block, axis, [(i, i ^ bit) for i in range(count)])


def fill_slots(codes_ref, rows, out_ref, first):
    queries = rows.shape[0]
    codes = codes_ref[...]
    slot = lax.broadcasted_iota(jnp.int32, (2 * CAP, queries), 0).astype(jnp.int16)
    one, zero = jnp.ones((), jnp.bfloat16), jnp.zeros((), jnp.bfloat16)
    for step in range(0, out_ref.shape[0], 2):
        near = (codes - (first + step) * CAP).astype(jnp.int16)
        hit = slot == near[0:1, :]
        for entry in range(1, codes.shape[0]):
            hit = hit | (slot == near[entry:entry + 1, :])
        got = jnp.dot(jnp.where(hit, one, zero), rows, preferred_element_type=jnp.float32).astype(jnp.bfloat16)
        out_ref[step:step + 2] = got.reshape(2, CAP, got.shape[1])


def project_kernel(codes_ref, queries_hbm, gain_hbm, weight_hbm, rows_ref, *refs):
    lower_ref, upper_ref, queries_ref, gain_ref, weight_ref, sems = refs
    copies = [
        pltpu.make_async_copy(source, target, sems.at[i])
        for i, (source, target) in enumerate(((queries_hbm, queries_ref), (gain_hbm, gain_ref), (weight_hbm, weight_ref)))
    ]
    for copy in copies:
        copy.start()
    for copy in copies:
        copy.wait()
    values = queries_ref[...].astype(jnp.float32)
    average = jnp.mean(values, axis=-1, keepdims=True)
    centred = values - average
    spread = jnp.mean(centred * centred, axis=-1, keepdims=True)
    normed = (centred * lax.rsqrt(spread + 1e-05) * gain_ref[...]).astype(jnp.bfloat16)
    rows = jnp.dot(normed, weight_ref[...], preferred_element_type=jnp.float32).astype(jnp.bfloat16)
    rows_ref[...] = rows
    fill_slots(codes_ref, rows, lower_ref, 2 * BLK_DEV)
    fill_slots(codes_ref, rows, upper_ref, 0)


def slot_shape(blocks, width):
    return jax.ShapeDtypeStruct((blocks, CAP, width), jnp.bfloat16)


def project(codes, queries, gain, weight, blocks):
    count, width = queries.shape
    hbm = pl.BlockSpec(memory_space=pltpu.HBM)
    return pl.pallas_call(
        project_kernel,
        in_specs=[pl.BlockSpec(memory_space=pltpu.VMEM), hbm, hbm, hbm],
        scratch_shapes=[
            pltpu.VMEM(queries.shape, queries.dtype),
            pltpu.VMEM(gain.shape, gain.dtype),
            pltpu.VMEM(weight.shape, weight.dtype),
            pltpu.SemaphoreType.DMA((3,)),
        ],
        out_shape=(jax.ShapeDtypeStruct((count, width), jnp.bfloat16),) + (slot_shape(blocks, width),) * 2,
        compiler_params=params(),
        cost_estimate=pl.CostEstimate(flops=4 << 30, bytes_accessed=2 << 20, transcendentals=0),
        name="project",
    )(codes, queries, gain, weight)


def scatter_kernel(codes_ref, rows_ref, own_ref, *refs, blocks):
    rows = rows_ref[...]
    for ref, first in zip(refs, (2 * BLK_DEV + blocks, blocks)):
        fill_slots(codes_ref, rows, ref, first)
    fill_slots(codes_ref, rows, own_ref, BLK_DEV)


def scatter(codes, rows, blocks):
    width = rows.shape[1]
    rest = BLK_DEV - blocks
    return pl.pallas_call(
        functools.partial(scatter_kernel, blocks=blocks),
        out_shape=(slot_shape(BLK_DEV, width),) + ((slot_shape(rest, width),) * 2 if rest else ()),
        compiler_params=params(),
        cost_estimate=pl.CostEstimate(flops=1 << 30, bytes_accessed=2 << 20, transcendentals=0),
        name="scatter",
    )(codes, rows)


def kv_kernel(key_ref, value_ref, *refs):
    out_ref = refs[-1]
    keys, width = out_ref.shape[1], key_ref.shape[1]
    done = 0
    for ref in refs[:-1]:
        for at in range(0, ref.shape[0], keys):
            rows = ref[at:at + keys]
            for side, weight_ref in enumerate((key_ref, value_ref)):
                got = jnp.dot(rows, weight_ref[...], preferred_element_type=jnp.float32)
                out_ref[done, :, side * width:(side + 1) * width] = got.astype(jnp.bfloat16)
            done += 1


def keys_and_values(features, w_key, w_value, keys):
    width = w_key.shape[1]
    count = sum(part.shape[0] for part in features)
    return pl.pallas_call(
        kv_kernel,
        out_shape=jax.ShapeDtypeStruct((count // keys, keys, 2 * width), jnp.bfloat16),
        compiler_params=params(),
        cost_estimate=pl.CostEstimate(flops=4 * count * width * width, bytes_accessed=6 * count * width, transcendentals=0),
        name="keys_and_values",
    )(w_key, w_value, *features)


def attend_kernel(rows_ref, kv_ref, out_ref, scores_ref, *, stack, start, unroll):
    blocks, (_, count, width) = kv_ref.shape[0], rows_ref.shape
    head_size = width // HEADS
    factor = head_size ** (-0.5) * LOG2_E
    head_of = lax.broadcasted_iota(jnp.int32, (1, width), 1) // head_size
    firsts = list(range(0, HEADS, stack))
    half = width // 2

    def scores_of(b, first):
        side = slice(half * (first >= HEADS // 2), half * (first >= HEADS // 2) + half)
        rows = rows_ref[start + b, :, side]
        kept = [jnp.where(head_of[:, side] == first + i, rows, jnp.zeros_like(rows)) for i in range(stack)]
        return lax.dot_general(
            jnp.concatenate(kept, axis=0), kv_ref[b, :, side],
            (((1,), (1,)), ((), ())), preferred_element_type=jnp.float32)

    def visit(step, scores, closing):
        for unit in range(unroll):
            b = step * unroll + unit
            merged = None
            for at, first in enumerate(firsts):
                if at + 1 < len(firsts):
                    following = scores_of(b, firsts[at + 1])
                elif closing and unit + 1 == unroll:
                    following = None
                else:
                    following = scores_of(jnp.minimum(b + 1, blocks - 1), 0)
                peak = jnp.max(scores, axis=1, keepdims=True)
                expo = jnp.exp2((scores - peak) * factor)
                weights = (expo * (1.0 / jnp.sum(expo, axis=1, keepdims=True))).astype(jnp.bfloat16)
                got = jnp.dot(weights, kv_ref[b, :, width:], preferred_element_type=jnp.float32)
                for i in range(stack):
                    part = got[i * count:(i + 1) * count]
                    merged = part if first + i == 0 else jnp.where(head_of == first + i, part, merged)
                scores = following
            out_ref[b] = merged.astype(jnp.bfloat16)
        return scores

    if unroll == blocks:
        visit(0, scores_of(0, 0), True)
        return
    scores_ref[...] = scores_of(0, 0)

    @pl.loop(0, blocks // unroll)
    def _(step):
        scores_ref[...] = visit(step, scores_ref[...], False)


def attend(rows, kv, start=0, unroll=UNROLL):
    _, count, width = rows.shape
    blocks, keys = kv.shape[:2]
    stack = 2
    pairs = blocks * count * keys
    return pl.pallas_call(
        functools.partial(attend_kernel, stack=stack, start=start, unroll=unroll),
        out_shape=jax.ShapeDtypeStruct((blocks, count, width), jnp.bfloat16),
        scratch_shapes=[pltpu.VMEM((stack * count, keys), jnp.float32)],
        compiler_params=params(),
        cost_estimate=pl.CostEstimate(
            flops=4 * pairs * width * HEADS, bytes_accessed=blocks * keys * width * 4,
            transcendentals=pairs * HEADS),
        name="attend",
    )(rows, kv)


def pick_kernel(codes_ref, *out_refs, groups):
    entries, count = codes_ref.shape
    spare = jnp.zeros((8 - entries, count), jnp.int32)
    at = jnp.concatenate([codes_ref[...], spare], axis=0).T
    tile = 16
    lane = lax.broadcasted_iota(jnp.int32, (1, tile, CAP), 2).astype(jnp.int16)
    near = [
        jnp.broadcast_to(at[:, entry:entry + 1], (count, CAP)).astype(jnp.int16).reshape(count // tile, tile, CAP)
        for entry in range(entries)
    ]
    one, zero = jnp.ones((), jnp.bfloat16), jnp.zeros((), jnp.bfloat16)
    for group, out_ref in zip(groups, out_refs):
        for step in range(out_ref.shape[1] // CAP):
            slot = lane + jnp.int16(group * BLK_DEV * CAP + step * CAP)
            hit = slot == near[0]
            for entry in range(1, entries):
                hit = hit | (slot == near[entry])
            out_ref[:, step * CAP:(step + 1) * CAP] = jnp.where(hit, one, zero).reshape(count, CAP)


def picks(codes, groups):
    shape = jax.ShapeDtypeStruct((codes.shape[1], BLK_DEV * CAP), jnp.bfloat16)
    return pl.pallas_call(
        functools.partial(pick_kernel, groups=groups),
        out_shape=(shape,) * len(groups),
        compiler_params=params(),
        cost_estimate=pl.CostEstimate(flops=1 << 30, bytes_accessed=2 << 20, transcendentals=0),
        name="picks",
    )(codes)


def gathered(pick_refs, result_refs, places, rows):
    total = None
    for ref, (group, first) in zip(result_refs, places):
        slots = ref.shape[0] * ref.shape[1]
        got = jnp.dot(
            pick_refs[group][rows, first:first + slots], ref[...].reshape(slots, ref.shape[2]),
            preferred_element_type=jnp.float32)
        total = got if total is None else total + got
    return total


def partial_kernel(*refs, places):
    pick_refs, result_refs, out_ref = refs[:3], refs[3:-1], refs[-1]
    tile = 256
    for step in range(out_ref.shape[0] // tile):
        rows = slice(step * tile, (step + 1) * tile)
        out_ref[rows] = gathered(pick_refs, result_refs, places, rows)


def partial_sum(selected, results, places):
    return pl.pallas_call(
        functools.partial(partial_kernel, places=places),
        out_shape=jax.ShapeDtypeStruct((selected[0].shape[0], results[0].shape[2]), jnp.float32),
        compiler_params=params(),
        cost_estimate=pl.CostEstimate(flops=1 << 30, bytes_accessed=2 << 20, transcendentals=0),
        name="partial_sum",
    )(*selected, *results)


def final_kernel(partial_ref, queries_ref, weight_ref, *refs, places):
    pick_refs, result_refs, out_ref = refs[:3], refs[3:-1], refs[-1]
    tile = 256
    for step in range(out_ref.shape[0] // tile):
        rows = slice(step * tile, (step + 1) * tile)
        total = partial_ref[rows] + gathered(pick_refs, result_refs, places, rows)
        final = jnp.dot(total.astype(jnp.bfloat16), weight_ref[...], preferred_element_type=jnp.float32)
        out_ref[rows] = (final + queries_ref[rows].astype(jnp.float32)).astype(jnp.bfloat16)


def finish(partial, queries, weight, selected, results, places):
    return pl.pallas_call(
        functools.partial(final_kernel, places=places),
        out_shape=jax.ShapeDtypeStruct(queries.shape, jnp.bfloat16),
        compiler_params=params(),
        cost_estimate=pl.CostEstimate(flops=1 << 30, bytes_accessed=2 << 20, transcendentals=0),
        name="finish",
    )(partial, queries, weight, *selected, *results)


def shards(queries, norm_gain, w_query, w_key, w_value, w_out, features, visible, live):
    azim_cells, range_cells, width = queries.shape
    entries = visible.shape[2]
    count = azim_cells * range_cells
    bands = lax.axis_size("band")
    local_rows = features.shape[0]
    keys = bands * local_rows // BLK_DEV
    staged = bands == 4 and local_rows == 2 * keys

    shift = (lax.axis_index("band") * local_rows // keys) * CAP
    span = BLK_DEV * CAP
    turned = visible + (2 - 2 * lax.div(visible, span)) * span
    named = jnp.where(lax.axis_index("sector") % 2 == 1, turned, visible)
    codes = jnp.where(live != 0, named ^ shift, -1).transpose(2, 0, 1).reshape(entries, count)
    rows_in = queries.reshape(count, width)

    if staged:
        across = swapped(features, "band", 2)
        held = [[features, swapped(features, "band", 1)]]
    else:
        whole_sector = features
        bit = 1
        while bit < bands:
            whole_sector = jnp.concatenate([whole_sector, swapped(whole_sector, "band", bit)], axis=0)
            bit *= 2
        held = [[whole_sector]]
    selected = picks(codes, (0, 1, 2))
    codes, *selected = lax.optimization_barrier((codes, *selected))
    blocks = BLK_DEV // 2 if staged else BLK_DEV
    projected, *ready = project(codes, rows_in, norm_gain.reshape(1, width), w_query, blocks)

    def send(lower, upper):
        lower = exchanged(lower, 0)
        return lower, exchanged(upper, 1)

    visits = [send(*ready)]
    projected, *_ = lax.optimization_barrier((projected, *ready))
    slots_own, *ready = scatter(codes, projected, blocks)
    kvs = [keys_and_values(held[0], w_key, w_value, keys)]
    own = [attend(slots_own, kvs[0], unroll=4 if staged else UNROLL)]
    last = own[0]
    if staged:
        *ready, last = lax.optimization_barrier((*ready, last))
        visits.append(send(*ready))
    back = []
    for part, (lower, upper) in enumerate(visits):
        if part:
            kvs.append(keys_and_values([across, beyond], w_key, w_value, keys))
        arrived = {"lower": lower, "upper": upper}
        turns = ("upper", "lower") if part else ("lower", "upper")
        for name in turns:
            rows, last = lax.optimization_barrier((arrived[name], last))
            last = arrived[name] = attend(rows, kvs[part])
        if staged and not part:
            *both, across = lax.optimization_barrier((*arrived.values(), across))
            arrived = dict(zip(arrived, both))
            beyond = swapped(across, "band", 1)
        for side, name in enumerate(("lower", "upper")):
            arrived[name] = exchanged(arrived[name], side)
        back.append((arrived["lower"], arrived["upper"]))
    if staged:
        turn, last = lax.optimization_barrier((slots_own, last))
        own.append(attend(turn, kvs[1], blocks, unroll=4))

    cuts = [i * blocks * CAP for i in range(len(kvs))]
    early = [((1, at), rows) for at, rows in zip(cuts, own)]
    returned = [((0, at), upper) for at, (_, upper) in zip(cuts, back)]
    returned += [((2, at), lower) for at, (lower, _) in zip(cuts, back)]
    early += returned[:-1]
    partial = partial_sum(selected, [rows for _, rows in early], tuple(at for at, _ in early))
    late = returned[-1:]
    out = finish(partial, rows_in, w_out, selected, [rows for _, rows in late], tuple(at for at, _ in late))
    return out.reshape(azim_cells, range_cells, width)


def solution(mesh):
    return jax.shard_map(
        shards,
        mesh=mesh,
        in_specs=(
            P("sector", "band", None),
            P(),
            P(),
            P(),
            P(),
            P(),
            P(("sector", "band"), None),
            P("sector", "band", None),
            P("sector", "band", None),
        ),
        out_specs=P("sector", "band", None),
        check_vma=False,
    )
```

```python
import functools

import jax
import jax.numpy as jnp
from jax import lax
from jax.experimental import pallas as pl
from jax.experimental.pallas import tpu as pltpu
from jax.sharding import PartitionSpec as P


HEADS = 8
BLK_DEV = 8
CAP = 128
LOG2_E = 1.4426950408889634
VMEM_BYTES = 24 << 20
UNROLL = 2


def params():
    return pltpu.CompilerParams(vmem_limit_bytes=VMEM_BYTES)


def exchanged(block, side):
    count = lax.axis_size("sector")
    return lax.ppermute(block, "sector", [(i, (((i + side) ^ 1) - side) % count) for i in range(count)])


def swapped(block, axis, bit):
    count = lax.axis_size(axis)
    return lax.ppermute(block, axis, [(i, i ^ bit) for i in range(count)])


def fill_slots(codes_ref, rows, out_ref, first):
    queries = rows.shape[0]
    codes = codes_ref[...]
    slot = lax.broadcasted_iota(jnp.int32, (2 * CAP, queries), 0).astype(jnp.int16)
    one, zero = jnp.ones((), jnp.bfloat16), jnp.zeros((), jnp.bfloat16)
    for step in range(0, out_ref.shape[0], 2):
        near = (codes - (first + step) * CAP).astype(jnp.int16)
        hit = slot == near[0:1, :]
        for entry in range(1, codes.shape[0]):
            hit = hit | (slot == near[entry:entry + 1, :])
        got = jnp.dot(jnp.where(hit, one, zero), rows, preferred_element_type=jnp.float32).astype(jnp.bfloat16)
        out_ref[step:step + 2] = got.reshape(2, CAP, got.shape[1])


def project_kernel(codes_ref, queries_hbm, gain_hbm, weight_hbm, rows_ref, *refs):
    lower_ref, upper_ref, queries_ref, gain_ref, weight_ref, sems = refs
    copies = [
        pltpu.make_async_copy(source, target, sems.at[i])
        for i, (source, target) in enumerate(((queries_hbm, queries_ref), (gain_hbm, gain_ref), (weight_hbm, weight_ref)))
    ]
    for copy in copies:
        copy.start()
    for copy in copies:
        copy.wait()
    values = queries_ref[...].astype(jnp.float32)
    average = jnp.mean(values, axis=-1, keepdims=True)
    centred = values - average
    spread = jnp.mean(centred * centred, axis=-1, keepdims=True)
    normed = (centred * lax.rsqrt(spread + 1e-05) * gain_ref[...]).astype(jnp.bfloat16)
    rows = jnp.dot(normed, weight_ref[...], preferred_element_type=jnp.float32).astype(jnp.bfloat16)
    rows_ref[...] = rows
    fill_slots(codes_ref, rows, lower_ref, 2 * BLK_DEV)
    fill_slots(codes_ref, rows, upper_ref, 0)


def slot_shape(blocks, width):
    return jax.ShapeDtypeStruct((blocks, CAP, width), jnp.bfloat16)


def project(codes, queries, gain, weight, blocks):
    count, width = queries.shape
    hbm = pl.BlockSpec(memory_space=pltpu.HBM)
    return pl.pallas_call(
        project_kernel,
        in_specs=[pl.BlockSpec(memory_space=pltpu.VMEM), hbm, hbm, hbm],
        scratch_shapes=[
            pltpu.VMEM(queries.shape, queries.dtype),
            pltpu.VMEM(gain.shape, gain.dtype),
            pltpu.VMEM(weight.shape, weight.dtype),
            pltpu.SemaphoreType.DMA((3,)),
        ],
        out_shape=(jax.ShapeDtypeStruct((count, width), jnp.bfloat16),) + (slot_shape(blocks, width),) * 2,
        compiler_params=params(),
        cost_estimate=pl.CostEstimate(flops=4 << 30, bytes_accessed=2 << 20, transcendentals=0),
        name="project",
    )(codes, queries, gain, weight)


def scatter_kernel(codes_ref, rows_ref, own_ref, *refs, blocks):
    rows = rows_ref[...]
    for ref, first in zip(refs, (2 * BLK_DEV + blocks, blocks)):
        fill_slots(codes_ref, rows, ref, first)
    fill_slots(codes_ref, rows, own_ref, BLK_DEV)


def scatter(codes, rows, blocks):
    width = rows.shape[1]
    rest = BLK_DEV - blocks
    return pl.pallas_call(
        functools.partial(scatter_kernel, blocks=blocks),
        out_shape=(slot_shape(BLK_DEV, width),) + ((slot_shape(rest, width),) * 2 if rest else ()),
        compiler_params=params(),
        cost_estimate=pl.CostEstimate(flops=1 << 30, bytes_accessed=2 << 20, transcendentals=0),
        name="scatter",
    )(codes, rows)


def kv_kernel(key_ref, value_ref, *refs):
    out_ref = refs[-1]
    keys, width = out_ref.shape[1], key_ref.shape[1]
    done = 0
    for ref in refs[:-1]:
        for at in range(0, ref.shape[0], keys):
            rows = ref[at:at + keys]
            for side, weight_ref in enumerate((key_ref, value_ref)):
                got = jnp.dot(rows, weight_ref[...], preferred_element_type=jnp.float32)
                out_ref[done, :, side * width:(side + 1) * width] = got.astype(jnp.bfloat16)
            done += 1


def keys_and_values(features, w_key, w_value, keys):
    width = w_key.shape[1]
    count = sum(part.shape[0] for part in features)
    return pl.pallas_call(
        kv_kernel,
        out_shape=jax.ShapeDtypeStruct((count // keys, keys, 2 * width), jnp.bfloat16),
        compiler_params=params(),
        cost_estimate=pl.CostEstimate(flops=4 * count * width * width, bytes_accessed=6 * count * width, transcendentals=0),
        name="keys_and_values",
    )(w_key, w_value, *features)


def attend_kernel(rows_ref, kv_ref, out_ref, scores_ref, *, stack, start):
    blocks, (_, count, width) = kv_ref.shape[0], rows_ref.shape
    head_size = width // HEADS
    factor = head_size ** (-0.5) * LOG2_E
    head_of = lax.broadcasted_iota(jnp.int32, (1, width), 1) // head_size
    firsts = list(range(0, HEADS, stack))
    half = width // 2

    def scores_of(b, first):
        side = slice(half * (first >= HEADS // 2), half * (first >= HEADS // 2) + half)
        rows = rows_ref[start + b, :, side]
        kept = [jnp.where(head_of[:, side] == first + i, rows, jnp.zeros_like(rows)) for i in range(stack)]
        return lax.dot_general(
            jnp.concatenate(kept, axis=0), kv_ref[b, :, side],
            (((1,), (1,)), ((), ())), preferred_element_type=jnp.float32)

    scores_ref[...] = scores_of(0, 0)

    @pl.loop(0, blocks // UNROLL)
    def _(step):
        scores = scores_ref[...]
        for unit in range(UNROLL):
            b = step * UNROLL + unit
            merged = None
            for at, first in enumerate(firsts):
                if at + 1 < len(firsts):
                    following = scores_of(b, firsts[at + 1])
                else:
                    following = scores_of(jnp.minimum(b + 1, blocks - 1), 0)
                peak = jnp.max(scores, axis=1, keepdims=True)
                expo = jnp.exp2((scores - peak) * factor)
                weights = (expo * (1.0 / jnp.sum(expo, axis=1, keepdims=True))).astype(jnp.bfloat16)
                got = jnp.dot(weights, kv_ref[b, :, width:], preferred_element_type=jnp.float32)
                for i in range(stack):
                    part = got[i * count:(i + 1) * count]
                    merged = part if first + i == 0 else jnp.where(head_of == first + i, part, merged)
                scores = following
            out_ref[b] = merged.astype(jnp.bfloat16)
        scores_ref[...] = scores


def attend(rows, kv, start=0):
    _, count, width = rows.shape
    blocks, keys = kv.shape[:2]
    stack = 2
    pairs = blocks * count * keys
    return pl.pallas_call(
        functools.partial(attend_kernel, stack=stack, start=start),
        out_shape=jax.ShapeDtypeStruct((blocks, count, width), jnp.bfloat16),
        scratch_shapes=[pltpu.VMEM((stack * count, keys), jnp.float32)],
        compiler_params=params(),
        cost_estimate=pl.CostEstimate(
            flops=4 * pairs * width * HEADS, bytes_accessed=blocks * keys * width * 4,
            transcendentals=pairs * HEADS),
        name="attend",
    )(rows, kv)


def pick_kernel(codes_ref, *out_refs, groups):
    entries, count = codes_ref.shape
    spare = jnp.zeros((8 - entries, count), jnp.int32)
    at = jnp.concatenate([codes_ref[...], spare], axis=0).T
    lane = lax.broadcasted_iota(jnp.int32, (count, CAP), 1).astype(jnp.int16)
    near = [jnp.broadcast_to(at[:, entry:entry + 1], (count, CAP)).astype(jnp.int16) for entry in range(entries)]
    one, zero = jnp.ones((), jnp.bfloat16), jnp.zeros((), jnp.bfloat16)
    for group, out_ref in zip(groups, out_refs):
        for step in range(out_ref.shape[1] // CAP):
            slot = lane + jnp.int16(group * BLK_DEV * CAP + step * CAP)
            hit = slot == near[0]
            for entry in range(1, entries):
                hit = hit | (slot == near[entry])
            out_ref[:, step * CAP:(step + 1) * CAP] = jnp.where(hit, one, zero)


def picks(codes, groups):
    shape = jax.ShapeDtypeStruct((codes.shape[1], BLK_DEV * CAP), jnp.bfloat16)
    return pl.pallas_call(
        functools.partial(pick_kernel, groups=groups),
        out_shape=(shape,) * len(groups),
        compiler_params=params(),
        cost_estimate=pl.CostEstimate(flops=1 << 30, bytes_accessed=2 << 20, transcendentals=0),
        name="picks",
    )(codes)


def gathered(pick_refs, result_refs, places, rows):
    total = None
    for ref, (group, first) in zip(result_refs, places):
        slots = ref.shape[0] * ref.shape[1]
        got = jnp.dot(
            pick_refs[group][rows, first:first + slots], ref[...].reshape(slots, ref.shape[2]),
            preferred_element_type=jnp.float32)
        total = got if total is None else total + got
    return total


def partial_kernel(*refs, places):
    pick_refs, result_refs, out_ref = refs[:3], refs[3:-1], refs[-1]
    tile = 256
    for step in range(out_ref.shape[0] // tile):
        rows = slice(step * tile, (step + 1) * tile)
        out_ref[rows] = gathered(pick_refs, result_refs, places, rows)


def partial_sum(selected, results, places):
    return pl.pallas_call(
        functools.partial(partial_kernel, places=places),
        out_shape=jax.ShapeDtypeStruct((selected[0].shape[0], results[0].shape[2]), jnp.float32),
        compiler_params=params(),
        cost_estimate=pl.CostEstimate(flops=1 << 30, bytes_accessed=2 << 20, transcendentals=0),
        name="partial_sum",
    )(*selected, *results)


def final_kernel(partial_ref, queries_ref, weight_ref, *refs, places):
    pick_refs, result_refs, out_ref = refs[:3], refs[3:-1], refs[-1]
    tile = 256
    for step in range(out_ref.shape[0] // tile):
        rows = slice(step * tile, (step + 1) * tile)
        total = partial_ref[rows] + gathered(pick_refs, result_refs, places, rows)
        final = jnp.dot(total.astype(jnp.bfloat16), weight_ref[...], preferred_element_type=jnp.float32)
        out_ref[rows] = (final + queries_ref[rows].astype(jnp.float32)).astype(jnp.bfloat16)


def finish(partial, queries, weight, selected, results, places):
    return pl.pallas_call(
        functools.partial(final_kernel, places=places),
        out_shape=jax.ShapeDtypeStruct(queries.shape, jnp.bfloat16),
        compiler_params=params(),
        cost_estimate=pl.CostEstimate(flops=1 << 30, bytes_accessed=2 << 20, transcendentals=0),
        name="finish",
    )(partial, queries, weight, *selected, *results)


def shards(queries, norm_gain, w_query, w_key, w_value, w_out, features, visible, live):
    azim_cells, range_cells, width = queries.shape
    entries = visible.shape[2]
    count = azim_cells * range_cells
    bands = lax.axis_size("band")
    local_rows = features.shape[0]
    keys = bands * local_rows // BLK_DEV
    staged = bands == 4 and local_rows == 2 * keys

    shift = (lax.axis_index("band") * local_rows // keys) * CAP
    span = BLK_DEV * CAP
    turned = visible + (2 - 2 * lax.div(visible, span)) * span
    named = jnp.where(lax.axis_index("sector") % 2 == 1, turned, visible)
    codes = jnp.where(live != 0, named ^ shift, -1).transpose(2, 0, 1).reshape(entries, count)
    rows_in = queries.reshape(count, width)

    if staged:
        across = swapped(features, "band", 2)
        held = [[features, swapped(features, "band", 1)]]
    else:
        whole_sector = features
        bit = 1
        while bit < bands:
            whole_sector = jnp.concatenate([whole_sector, swapped(whole_sector, "band", bit)], axis=0)
            bit *= 2
        held = [[whole_sector]]
    selected = picks(codes, (0, 1, 2))
    codes, *selected = lax.optimization_barrier((codes, *selected))
    blocks = BLK_DEV // 2 if staged else BLK_DEV
    projected, *ready = project(codes, rows_in, norm_gain.reshape(1, width), w_query, blocks)

    def send(lower, upper):
        lower = exchanged(lower, 0)
        return lower, exchanged(upper, 1)

    visits = [send(*ready)]
    projected, *_ = lax.optimization_barrier((projected, *ready))
    slots_own, *ready = scatter(codes, projected, blocks)
    kvs = [keys_and_values(held[0], w_key, w_value, keys)]
    own = [attend(slots_own, kvs[0])]
    last = own[0]
    if staged:
        *ready, last = lax.optimization_barrier((*ready, last))
        visits.append(send(*ready))
    back = []
    for part, (lower, upper) in enumerate(visits):
        if part:
            kvs.append(keys_and_values([across, beyond], w_key, w_value, keys))
        arrived = {"lower": lower, "upper": upper}
        turns = ("upper", "lower") if part else ("lower", "upper")
        for name in turns:
            rows, last = lax.optimization_barrier((arrived[name], last))
            last = arrived[name] = attend(rows, kvs[part])
        if staged and not part:
            *both, across = lax.optimization_barrier((*arrived.values(), across))
            arrived = dict(zip(arrived, both))
            beyond = swapped(across, "band", 1)
        for side, name in enumerate(("lower", "upper")):
            arrived[name] = exchanged(arrived[name], side)
        back.append((arrived["lower"], arrived["upper"]))
    if staged:
        turn, last = lax.optimization_barrier((slots_own, last))
        own.append(attend(turn, kvs[1], blocks))

    cuts = [i * blocks * CAP for i in range(len(kvs))]
    early = [((1, at), rows) for at, rows in zip(cuts, own)]
    returned = [((0, at), upper) for at, (_, upper) in zip(cuts, back)]
    returned += [((2, at), lower) for at, (lower, _) in zip(cuts, back)]
    early += returned[:-1]
    partial = partial_sum(selected, [rows for _, rows in early], tuple(at for at, _ in early))
    late = returned[-1:]
    out = finish(partial, rows_in, w_out, selected, [rows for _, rows in late], tuple(at for at, _ in late))
    return out.reshape(azim_cells, range_cells, width)


def solution(mesh):
    return jax.shard_map(
        shards,
        mesh=mesh,
        in_specs=(
            P("sector", "band", None),
            P(),
            P(),
            P(),
            P(),
            P(),
            P(("sector", "band"), None),
            P("sector", "band", None),
            P("sector", "band", None),
        ),
        out_specs=P("sector", "band", None),
        check_vma=False,
    )
```
